256 devices in a mesh: group: 8 (over y, x_hi), fsdp: 32 (over x_lo, z, core).
Axes of the slice: x: 4 (x_hi: 2, x_lo: 2; x = x_hi * 2 + x_lo), y: 4, z: 8, core: 2. Of those that a mesh axis runs over, the one named last changes fastest.
Arguments:
- inputs: bfloat16 [16384, 4096], P('group', 'fsdp'), may hold values from -6 to 6
- norm_gain: bfloat16 [4096], P('fsdp'), may hold values from 0.099609375 to 1.8984375
- cotangent: bfloat16 [16384, 16384], P('group', 'fsdp'), may hold values from -0.0234375 to 0.0234375
- owners: int32 [32, 8], P('fsdp'), may hold values from 0 to 7, each once within a row
- refresh: int32 [8, 32], P('group', 'fsdp'), may hold values 0 or 1
- left_stats: float32 [4096, 16384], P('group', 'fsdp'), may hold values from -1 to 16, as said below
- right_stats: float32 [4096, 16384], P('group', 'fsdp'), may hold values from -1 to 16, as said below
- left_inverse: float32 [4096, 16384], P('group', 'fsdp'), may hold values from -1 to 8, as said below
- right_inverse: float32 [4096, 16384], P('group', 'fsdp'), may hold values from -1 to 8, as said below
Outputs:
- update: bfloat16 [4096, 16384], P('group', 'fsdp')
- left_accum: float32 [4096, 16384], P('group', 'fsdp')
- right_accum: float32 [4096, 16384], P('group', 'fsdp')
- left_refreshed: float32 [4096, 16384], P('group', 'fsdp')
- right_refreshed: float32 [4096, 16384], P('group', 'fsdp')
The draws below stay inside these ranges and needn't reach their ends.
Inputs may be any that keep to these rules, and one draw needn't show every extreme that they name: Each row owners[c] is a permutation of 0 to 8 - 1. `left_stats`: symmetric within each 512 x 512 block, diagonal entries at least 1. `right_stats`: symmetric within each 512 x 512 block, diagonal entries at least 1. `left_inverse`: symmetric within each 512 x 512 block. `right_inverse`: symmetric within each 512 x 512 block.
All inputs are finite; a program needn't handle non-finite values. No bound on the sum of `refresh` on one device may be relied on, other than what follows from the above.
Results may differ from the reference program's by a relative error of at most 0.013.
Values may be sent and summed in bfloat16 or wider, within the bound.
No kernel may reach another device: no remote copies, remote signals or barrier semaphores. Data moves between devices by JAX's collectives and lax.ppermute only.
A program may use at most 128 MiB of HBM per device.

```python
import jax
import jax.numpy as jnp
from jax import lax

D = 4096
F = 16384
BLK = 512
TOK_ROW = 2048
ITERS = 2
TOKENS = 16384
ROW_BLOCKS = 8
COL_BLOCKS = 32
N_GROUP = 8


def symmetric_blocks(key, lowest, highest):
    block_order = BLK
    row_count = D // block_order
    col_count = F // block_order
    half_width = 0.98 * lowest / block_order
    off_diagonal = jax.random.uniform(jax.random.fold_in(key, 1), (row_count, block_order, col_count, block_order), jnp.float32, -half_width, half_width)
    off_diagonal = 0.5 * (off_diagonal + off_diagonal.transpose(0, 3, 2, 1))
    log_values = jax.random.uniform(jax.random.fold_in(key, 2), (row_count, block_order, col_count, 1), jnp.float32, jnp.log(lowest), jnp.log(highest))
    on_diagonal = lax.broadcasted_iota(jnp.int32, (1, block_order, 1, block_order), 1) == lax.broadcasted_iota(jnp.int32, (1, block_order, 1, block_order), 3)
    filled = jnp.where(on_diagonal, jnp.exp(log_values), off_diagonal)
    return filled.reshape(row_count * block_order, col_count * block_order)


def draw_left_stats(key, part):
    return symmetric_blocks(jax.random.fold_in(key, 11), 1.0, 4.0)


def draw_right_stats(key, part):
    return symmetric_blocks(jax.random.fold_in(key, 12), 1.0, 4.0)


def draw_left_inverse(key, part):
    return symmetric_blocks(jax.random.fold_in(key, 13), 0.5, 2.0)


def draw_right_inverse(key, part):
    return symmetric_blocks(jax.random.fold_in(key, 14), 0.5, 2.0)


def touch_ends(entries, own_key, low, largest):
    longest = entries.shape.index(max(entries.shape))
    spots = []
    for shift in (0, 1):
        where = [jax.random.randint(jax.random.fold_in(own_key, axis), (), 0, length) for axis, length in enumerate(entries.shape)]
        where[longest] = (where[longest] + shift) % entries.shape[longest]
        spots.append(tuple(where))
    return entries.at[spots[0]].set(low).at[spots[1]].set(largest)


def shard_levels(stream_key, extent, pieces, least, largest):
    loudness = 1.0
    for position, shards_of in pieces:
        draws = jax.random.uniform(jax.random.fold_in(jax.random.fold_in(stream_key, 6), position), (shards_of,), jnp.float32, least / len(pieces), largest / len(pieces))
        loudness = loudness * jnp.repeat(jnp.exp(draws), extent[position] // shards_of).reshape((-1,) + (1,) * (len(extent) - 1 - position))
    return loudness


def gaussian(key, extent, scale, reach, pieces=(), kind=jnp.bfloat16):
    gain = shard_levels(key, extent, pieces, -0.22, 0.18) if pieces else 1.0
    entries = jax.random.normal(key, extent, jnp.float32) * scale * gain
    return jnp.minimum(jnp.maximum(entries, -reach), reach).astype(kind)


def setup_inputs(seed: int = 0) -> dict:
    key_of = jax.random.split(jax.random.key(seed), 10)
    return {
        "inputs": gaussian(key_of[0], (TOKENS, D), 1.0, 6.0, ((0, 8), (1, 32))),
        "norm_gain": jnp.clip(1.0 + 0.18 * jax.random.normal(key_of[1], (D,), jnp.float32), 0.099609375, 1.8984375).astype(jnp.bfloat16),
        "cotangent": gaussian(key_of[2], (TOKENS, F), ((25 * TOKENS) ** -0.5), 0.0234375, ((0, 8), (1, 32))),
        "owners": jax.vmap(lambda own: jax.random.permutation(own, N_GROUP))(jax.random.split(key_of[3], COL_BLOCKS)).reshape((COL_BLOCKS, N_GROUP)).astype(jnp.int32),
        "refresh": touch_ends((jax.random.randint(key_of[4], (ROW_BLOCKS, COL_BLOCKS), 0, 4) < 1).astype(jnp.int32), jax.random.fold_in(key_of[4], 1), 0, 1),
        "left_stats": draw_left_stats(jax.random.fold_in(key_of[9], 71), 0),
        "right_stats": draw_right_stats(jax.random.fold_in(key_of[9], 71), 0),
        "left_inverse": draw_left_inverse(jax.random.fold_in(key_of[9], 71), 0),
        "right_inverse": draw_right_inverse(jax.random.fold_in(key_of[9], 71), 0),
    }


NORM_EPSILON = 1e-05
SCALE_EPSILON = 1e-06
DECAY_RATE = 0.95
RIDGE_TERM = 1e-06
HIGHEST = lax.Precision.HIGHEST

def to_blocks(matrix, block_order):
    row_count, col_count = matrix.shape
    shaped = matrix.reshape(row_count // block_order, block_order, col_count // block_order, block_order)
    return shaped.transpose(0, 2, 1, 3).reshape(-1, block_order, block_order)

def from_blocks(blocks, row_count, col_count):
    block_order = blocks.shape[-1]
    shaped = blocks.reshape(row_count // block_order, col_count // block_order, block_order, block_order)
    return shaped.transpose(0, 2, 1, 3).reshape(row_count, col_count)

def inverse_fourth_root(statistic):
    block_order = statistic.shape[0]
    identity = jnp.eye(block_order, dtype=statistic.dtype)
    matrix = statistic + RIDGE_TERM * identity
    scaling = 2.5 / jnp.sqrt(jnp.sum(matrix * matrix))
    inverse_root = scaling ** 0.25 * identity
    scaled = scaling * matrix
    for iteration in range(ITERS):
        factor = 1.25 * identity - 0.25 * scaled
        inverse_root = jnp.dot(inverse_root, factor, precision=HIGHEST)
        if iteration + 1 < ITERS:
            square = jnp.dot(factor, factor, precision=HIGHEST)
            scaled = jnp.dot(jnp.dot(square, square, precision=HIGHEST), scaled, precision=HIGHEST)
    return inverse_root

def block_step(operands):
    grad_block, left_old, right_old, left_root, right_root, refresh_flag = operands
    left_gram = lax.dot_general(grad_block, grad_block, (((1,), (1,)), ((), ())), preferred_element_type=jnp.float32)
    right_gram = lax.dot_general(grad_block, grad_block, (((0,), (0,)), ((), ())), preferred_element_type=jnp.float32)
    left_accum = DECAY_RATE * left_old + (1.0 - DECAY_RATE) * left_gram
    right_accum = DECAY_RATE * right_old + (1.0 - DECAY_RATE) * right_gram
    local_grad = grad_block.astype(jnp.float32)
    conditioned = jnp.dot(jnp.dot(left_root, local_grad, precision=HIGHEST), right_root, precision=HIGHEST)
    own_update = (conditioned * lax.rsqrt(jnp.mean(conditioned * conditioned) + SCALE_EPSILON)).astype(jnp.bfloat16)

    def recompute(unused):
        return (inverse_fourth_root(left_accum), inverse_fourth_root(right_accum))

    def keep_old(unused):
        return (left_root, right_root)
    left_new, right_new = lax.cond(refresh_flag > 0, recompute, keep_old, 0)
    return (own_update, left_accum, right_accum, left_new, right_new)

def reference(inputs, norm_gain, cotangent, owners, refresh, left_stats, right_stats, left_inverse, right_inverse):
    values = inputs.astype(jnp.float32)
    scales = lax.rsqrt(lax.optimization_barrier(jnp.mean(values * values, axis=1)) + NORM_EPSILON)
    normed = (values * scales[:, None] * norm_gain.astype(jnp.float32)[None, :]).astype(jnp.bfloat16)
    summed = jnp.zeros((D, F), jnp.float32)
    for group_row in range(N_GROUP):
        rows_in = normed[group_row * TOK_ROW:(group_row + 1) * TOK_ROW]
        grads_in = cotangent[group_row * TOK_ROW:(group_row + 1) * TOK_ROW]
        partial_value = lax.dot_general(rows_in, grads_in, (((0,), (0,)), ((), ())), preferred_element_type=jnp.float32)
        summed = summed + partial_value.astype(jnp.bfloat16).astype(jnp.float32)
    gradient = summed.astype(jnp.bfloat16)
    slab_rows = D // N_GROUP
    col_blocks = F // BLK
    rank_list = jnp.arange(N_GROUP, dtype=jnp.int32)
    inverse_map = lax.optimization_barrier(jnp.sum(jnp.where(owners[:, :, None] == rank_list[None, None, :], rank_list[None, :, None], 0), axis=1)).astype(jnp.int32)
    slab_shape = (N_GROUP, slab_rows, col_blocks, BLK)
    gather_index = jnp.broadcast_to(inverse_map.T[:, None, :, None], slab_shape)
    own_grad = jnp.take_along_axis(gradient.reshape(slab_shape), gather_index, axis=0).reshape(D, F)
    results = lax.map(block_step, (to_blocks(own_grad, BLK), to_blocks(left_stats, BLK), to_blocks(right_stats, BLK), to_blocks(left_inverse, BLK), to_blocks(right_inverse, BLK), refresh.reshape(-1)))
    own_update, left_accum, right_accum, left_new, right_new = results
    own_update = from_blocks(own_update, D, F)
    back_index = jnp.broadcast_to(owners.astype(jnp.int32).T[:, None, :, None], slab_shape)
    update = jnp.take_along_axis(own_update.reshape(slab_shape), back_index, axis=0).reshape(D, F)
    return (update, from_blocks(left_accum, D, F), from_blocks(right_accum, D, F), from_blocks(left_new, D, F), from_blocks(right_new, D, F))
```

```python
import jax
import jax.numpy as jnp
from jax import lax
from jax.experimental import pallas as pl
from jax.experimental.pallas import tpu as pltpu
from jax.sharding import Mesh
from jax.sharding import PartitionSpec as P

NORM_EPSILON = 1e-05
SCALE_EPSILON = 1e-06
DECAY_RATE = 0.95
RIDGE_TERM = 1e-06
BLK = 512
ITERS = 2
N_GROUP = 8
CHUNK = BLK // N_GROUP
GROUP = ("y", "xh")
FSDP = ("xl", "z", "core")
BF16 = jnp.bfloat16
F32 = jnp.float32
NT = (((1,), (1,)), ((), ()))
TN = (((0,), (0,)), ((), ()))


def dot(a, b):
    return jnp.dot(a, b, preferred_element_type=F32)


def dot_dims(a, b, dims):
    return lax.dot_general(a, b, dims, preferred_element_type=F32)


def split2(a):
    high = a.astype(BF16)
    return high, (a - high.astype(F32)).astype(BF16)


def transpose_kernel(x_ref, o_ref):
    o_ref[...] = x_ref[...].T


def transposed(x):
    rows, cols = x.shape
    return pl.pallas_call(
        transpose_kernel,
        grid=(rows // BLK,),
        in_specs=[pl.BlockSpec((BLK, cols), lambda i: (i, 0))],
        out_specs=pl.BlockSpec((cols, BLK), lambda i: (0, i)),
        out_shape=jax.ShapeDtypeStruct((cols, rows), x.dtype),
        name="transpose",
    )(x)


def pick_kernel(idx_ref, x_ref, o_ref):
    o_ref[...] = x_ref[...]


def pick(x, idx):
    rest = x.shape[1:]
    return pl.pallas_call(
        pick_kernel,
        grid_spec=pltpu.PrefetchScalarGridSpec(
            num_scalar_prefetch=1,
            grid=(x.shape[0],),
            in_specs=[pl.BlockSpec((1, *rest), lambda i, idx: (idx[i], 0, 0, 0))],
            out_specs=pl.BlockSpec((1, *rest), lambda i, idx: (i, 0, 0, 0)),
        ),
        out_shape=jax.ShapeDtypeStruct(x.shape, x.dtype),
        name="pick",
    )(idx, x)


def partial_kernel(cot_ref, x_ref, gain_ref, o_ref):
    x = jnp.concatenate([x_ref[i] for i in range(4)], axis=1)
    for half in range(2):
        rows = dot(cot_ref[half * BLK : (half + 1) * BLK, :], x)
        rows = (rows * gain_ref[0]).astype(BF16)
        for j in range(N_GROUP):
            o_ref[j, half, 0] = rows[j * CHUNK : (j + 1) * CHUNK]


def partials(cot, x, gain):
    tokens = cot.shape[1]
    slabs = x.shape[0] // 4
    flops = 2 * cot.shape[0] * tokens * slabs * BLK
    return pl.pallas_call(
        partial_kernel,
        grid=(slabs,),
        in_specs=[
            pl.BlockSpec((2 * BLK, tokens), lambda i: (0, 0)),
            pl.BlockSpec((4, tokens, 128), lambda i: (i, 0, 0)),
            pl.BlockSpec((1, 1, BLK), lambda i: (i, 0, 0)),
        ],
        out_specs=pl.BlockSpec((N_GROUP, 2, 1, CHUNK, BLK), lambda i: (0, 0, i, 0, 0)),
        out_shape=jax.ShapeDtypeStruct((N_GROUP, 2, slabs, CHUNK, BLK), BF16),
        compiler_params=pltpu.CompilerParams(vmem_limit_bytes=48 * 2**20),
        cost_estimate=pl.CostEstimate(flops=flops, bytes_accessed=16 * 2**20, transcendentals=0),
        name="partials",
    )(cot, x, gain)


def reduce_kernel(owner_ref, x_ref, o_ref):
    slab = pl.program_id(0)
    total = x_ref[0, 0].astype(F32)
    for g in range(1, N_GROUP):
        total = total + x_ref[g, 0].astype(F32)
    total = total.astype(BF16)
    o_ref[slab, 1] = total
    o_ref[owner_ref[slab], 0] = total


def reduce_route(x, owner):
    return pl.pallas_call(
        reduce_kernel,
        grid_spec=pltpu.PrefetchScalarGridSpec(
            num_scalar_prefetch=1,
            grid=(N_GROUP,),
            in_specs=[pl.BlockSpec((N_GROUP, 1, CHUNK, BLK), lambda i, owner: (0, i, 0, 0))],
            out_specs=pl.BlockSpec((N_GROUP, 2, CHUNK, BLK), lambda i, owner: (0, 0, 0, 0)),
        ),
        out_shape=jax.ShapeDtypeStruct((N_GROUP, 2, CHUNK, BLK), BF16),
        name="reduce_route",
    )(owner, x)


def inverse_fourth_root(statistic, eye):
    matrix = statistic + RIDGE_TERM * eye
    scaling = 2.5 * lax.rsqrt(jnp.sum(matrix * matrix, keepdims=True))
    scaled = scaling * matrix
    factor = 1.25 * eye - 0.25 * scaled
    rounded = factor.astype(BF16)
    square = dot(rounded, rounded).astype(BF16)
    fourth = dot(square, square).astype(BF16)
    scaled = dot(fourth, scaled.astype(BF16))
    second = 1.25 * eye - 0.25 * scaled
    root = jnp.sqrt(jnp.sqrt(scaling))
    return root * dot(rounded, second.astype(BF16))


def block_kernel(
    refresh_ref, g_ref, r_ref, ls_ref, rs_ref, li_ref, ri_ref, upd_ref, la_ref, ra_ref, ln_ref, rn_ref
):
    grad_t = g_ref[:, 0].reshape(BLK, BLK)
    left_accum = DECAY_RATE * ls_ref[...] + (1.0 - DECAY_RATE) * dot_dims(grad_t, grad_t, TN)
    right_accum = DECAY_RATE * rs_ref[...] + (1.0 - DECAY_RATE) * dot_dims(grad_t, grad_t, NT)
    la_ref[...] = left_accum
    ra_ref[...] = right_accum

    left_root = r_ref[:, 0].reshape(BLK, BLK)
    right_root = r_ref[:, 1].reshape(BLK, BLK)
    high, low = split2(dot_dims(left_root, g_ref[:, 1].reshape(BLK, BLK), NT))
    conditioned = dot(high, right_root) + dot(low, right_root)
    mean = jnp.sum(conditioned * conditioned, keepdims=True) * (1.0 / (BLK * BLK))
    upd_ref[...] = (conditioned * lax.rsqrt(mean + SCALE_EPSILON)).astype(BF16)

    @pl.when(refresh_ref[0, 0] > 0)
    def _():
        rows = lax.broadcasted_iota(jnp.int32, (BLK, BLK), 0)
        cols = lax.broadcasted_iota(jnp.int32, (BLK, BLK), 1)
        eye = (rows == cols).astype(F32)
        ln_ref[...] = inverse_fourth_root(la_ref[...], eye)
        rn_ref[...] = inverse_fourth_root(ra_ref[...], eye)

    @pl.when(refresh_ref[0, 0] <= 0)
    def _():
        ln_ref[...] = li_ref[...]
        rn_ref[...] = ri_ref[...]


def block_step(refresh, grads, roots, left_stats, right_stats, left_inverse, right_inverse):
    vmem = pl.BlockSpec(memory_space=pltpu.VMEM)
    square = jax.ShapeDtypeStruct((BLK, BLK), F32)
    return pl.pallas_call(
        block_kernel,
        in_specs=[pl.BlockSpec(memory_space=pltpu.SMEM)] + [vmem] * 6,
        out_specs=[vmem] * 5,
        out_shape=[jax.ShapeDtypeStruct((BLK, BLK), BF16)] + [square] * 4,
        compiler_params=pltpu.CompilerParams(vmem_limit_bytes=48 * 2**20),
        cost_estimate=pl.CostEstimate(flops=2**31, bytes_accessed=11 * 2**20, transcendentals=0),
        name="block_step",
    )(refresh, grads, roots, left_stats, right_stats, left_inverse, right_inverse)


def body(inputs, norm_gain, cotangent, owners, refresh, left_stats, right_stats, left_inverse, right_inverse):
    xl = lax.axis_index("xl")
    owner = owners[0]
    fsdp = lax.axis_size(FSDP)
    tokens, width = inputs.shape

    features = lax.all_gather(inputs, ("z", "core"), axis=0, tiled=False)

    cot_own = transposed(cotangent)
    cot_other = lax.ppermute(cot_own, "xl", [(0, 1), (1, 0)])

    values = inputs.astype(F32)
    squares = jnp.sum(values * values, axis=1)
    notes = jnp.concatenate([squares, norm_gain.astype(F32)])
    notes = jnp.broadcast_to(notes, (fsdp, 1, tokens + width))
    notes = lax.all_to_all(notes, FSDP, split_axis=0, concat_axis=0, tiled=True)[:, 0]
    scales = lax.rsqrt(jnp.sum(notes[:, :tokens], axis=0) / (fsdp * width) + NORM_EPSILON)
    gains = notes[:, tokens:].reshape(2, N_GROUP // 2, 1, BLK)
    gain = lax.dynamic_index_in_dim(gains, xl, 0, keepdims=False)

    roots = jnp.stack(
        [left_inverse.reshape(N_GROUP, CHUNK, BLK), right_inverse.reshape(N_GROUP, CHUNK, BLK)], axis=1
    ).astype(BF16)
    roots = lax.all_to_all(roots, GROUP, split_axis=0, concat_axis=0, tiled=True)
    roots = pick(roots, owner)
    roots = lax.all_to_all(roots, GROUP, split_axis=0, concat_axis=0, tiled=True)

    first = xl == 0
    cot = jnp.concatenate([jnp.where(first, cot_own, cot_other), jnp.where(first, cot_other, cot_own)], axis=0)
    cot = (cot.astype(F32) * scales[None, :]).astype(BF16)

    pieces = partials(cot, features, gain)
    pieces = pieces.reshape(2 * N_GROUP, N_GROUP // 2, CHUNK, BLK)
    pieces = lax.all_to_all(pieces, ("y", "xh", "xl"), split_axis=0, concat_axis=0, tiled=True)
    grads = reduce_route(pieces.reshape(N_GROUP, N_GROUP, CHUNK, BLK), owner)
    grads = lax.all_to_all(grads, GROUP, split_axis=0, concat_axis=0, tiled=True)
    return tuple(
        block_step(refresh, grads, roots, left_stats, right_stats, left_inverse, right_inverse)
    )


def solution(mesh):
    split = Mesh(mesh.devices.reshape(4, 2, 2, 8, 2), ("y", "xh", "xl", "z", "core"))
    both = P(GROUP, FSDP)
    in_specs = (both, P(FSDP), both, P(FSDP, None), both, both, both, both, both)
    return jax.shard_map(body, mesh=split, in_specs=in_specs, out_specs=(both,) * 5, check_vma=False)
```

```python
import jax
import jax.numpy as jnp
from jax import lax
from jax.experimental import pallas as pl
from jax.experimental.pallas import tpu as pltpu
from jax.sharding import Mesh
from jax.sharding import PartitionSpec as P

NORM_EPSILON = 1e-05
SCALE_EPSILON = 1e-06
DECAY_RATE = 0.95
RIDGE_TERM = 1e-06
BLK = 512
ITERS = 2
N_GROUP = 8
CHUNK = BLK // N_GROUP
GROUP = ("y", "xh")
FSDP = ("xl", "z", "core")
BF16 = jnp.bfloat16
F32 = jnp.float32
NT = (((1,), (1,)), ((), ()))
TN = (((0,), (0,)), ((), ()))


def dot(a, b):
    return jnp.dot(a, b, preferred_element_type=F32)


def dot_dims(a, b, dims):
    return lax.dot_general(a, b, dims, preferred_element_type=F32)


def split2(a):
    high = a.astype(BF16)
    return high, (a - high.astype(F32)).astype(BF16)


def prepare_kernel(x_ref, gain_ref, xt_ref, sq_ref):
    values = x_ref[...].astype(F32)
    xt_ref[...] = (values * gain_ref[...].astype(F32)).T.astype(BF16)
    sq_ref[...] = jnp.sum((values * values).T, axis=0, keepdims=True)


def prepare(x, gain):
    tokens, width = x.shape
    return pl.pallas_call(
        prepare_kernel,
        grid=(tokens // BLK,),
        in_specs=[pl.BlockSpec((BLK, width), lambda i: (i, 0)), pl.BlockSpec((1, width), lambda i: (0, 0))],
        out_specs=[pl.BlockSpec((width, BLK), lambda i: (0, i)), pl.BlockSpec((1, BLK), lambda i: (0, i))],
        out_shape=[jax.ShapeDtypeStruct((width, tokens), BF16), jax.ShapeDtypeStruct((1, tokens), F32)],
        name="prepare",
    )(x, gain.reshape(1, width))


def stack_roots_kernel(l_ref, r_ref, o_ref):
    o_ref[0, 0] = l_ref[...].astype(BF16)
    o_ref[0, 1] = r_ref[...].astype(BF16)


def stack_roots(left, right):
    rows = pl.BlockSpec((CHUNK, BLK), lambda i: (i, 0))
    return pl.pallas_call(
        stack_roots_kernel,
        grid=(N_GROUP,),
        in_specs=[rows, rows],
        out_specs=pl.BlockSpec((1, 2, CHUNK, BLK), lambda i: (i, 0, 0, 0)),
        out_shape=jax.ShapeDtypeStruct((N_GROUP, 2, CHUNK, BLK), BF16),
        name="stack_roots",
    )(left, right)


def pick_kernel(idx_ref, x_ref, o_ref):
    o_ref[...] = x_ref[...]


def pick(x, idx):
    rest = x.shape[1:]
    return pl.pallas_call(
        pick_kernel,
        grid_spec=pltpu.PrefetchScalarGridSpec(
            num_scalar_prefetch=1,
            grid=(x.shape[0],),
            in_specs=[pl.BlockSpec((1, *rest), lambda i, idx: (idx[i], 0, 0, 0))],
            out_specs=pl.BlockSpec((1, *rest), lambda i, idx: (i, 0, 0, 0)),
        ),
        out_shape=jax.ShapeDtypeStruct(x.shape, x.dtype),
        name="pick",
    )(idx, x)


def partial_kernel(xl_ref, x_ref, scale_ref, own_ref, other_ref, o_ref):
    rows = (x_ref[...].astype(F32) * scale_ref[...]).astype(BF16)
    for cot_ref, place in ((own_ref, xl_ref[0]), (other_ref, 1 - xl_ref[0])):
        part = dot(rows, cot_ref[...]).astype(BF16)
        for j in range(N_GROUP):
            o_ref[j, place, 0] = part[j * CHUNK : (j + 1) * CHUNK]


def partials(xl, x, scale, own, other, half):
    tokens = x.shape[1]
    whole = pl.BlockSpec((tokens, BLK), lambda i, xl: (0, 0))
    return pl.pallas_call(
        partial_kernel,
        grid_spec=pltpu.PrefetchScalarGridSpec(
            num_scalar_prefetch=1,
            grid=(2,),
            in_specs=[
                pl.BlockSpec((BLK, tokens), lambda i, xl: (2 * half + i, 0)),
                pl.BlockSpec((1, tokens), lambda i, xl: (0, 0)),
                whole,
                whole,
            ],
            out_specs=pl.BlockSpec((N_GROUP, 2, 1, CHUNK, BLK), lambda i, xl: (0, 0, i, 0, 0)),
        ),
        out_shape=pltpu.HBM((N_GROUP, 2, 2, CHUNK, BLK), BF16),
        compiler_params=pltpu.CompilerParams(vmem_limit_bytes=48 * 2**20),
        cost_estimate=pl.CostEstimate(flops=8 * tokens * BLK * BLK, bytes_accessed=10 * 2**20, transcendentals=0),
        name="partials",
    )(xl, x, scale, own, other)


def total(x_ref):
    acc = x_ref[0, 0, 0].astype(F32)
    for g in range(1, N_GROUP):
        acc = acc + x_ref[g, 0, 0].astype(F32)
    return acc.astype(BF16)


def reduce_kernel(x_ref, o_ref):
    o_ref[0] = total(x_ref)


def reduce_half(x):
    return pl.pallas_call(
        reduce_kernel,
        grid=(4,),
        in_specs=[pl.BlockSpec((N_GROUP, 1, 1, CHUNK, BLK), lambda i: (0, i // 2, i % 2, 0, 0))],
        out_specs=pl.BlockSpec((1, CHUNK, BLK), lambda i: (i, 0, 0)),
        out_shape=jax.ShapeDtypeStruct((4, CHUNK, BLK), BF16),
        name="reduce_half",
    )(x)


def route_kernel(owner_ref, first_ref, x_ref, o_ref):
    i = pl.program_id(0)

    def place(slab, value):
        o_ref[slab, 1] = value
        o_ref[owner_ref[slab], 0] = value

    slab = 4 * (i // 2) + i % 2
    place(slab, first_ref[0])
    place(slab + 2, total(x_ref))


def reduce_route(first, x, owner):
    return pl.pallas_call(
        route_kernel,
        grid_spec=pltpu.PrefetchScalarGridSpec(
            num_scalar_prefetch=1,
            grid=(4,),
            in_specs=[
                pl.BlockSpec((1, CHUNK, BLK), lambda i, owner: (i, 0, 0)),
                pl.BlockSpec((N_GROUP, 1, 1, CHUNK, BLK), lambda i, owner: (0, i // 2, i % 2, 0, 0)),
            ],
            out_specs=pl.BlockSpec((N_GROUP, 2, CHUNK, BLK), lambda i, owner: (0, 0, 0, 0)),
        ),
        out_shape=pltpu.HBM((N_GROUP, 2, CHUNK, BLK), BF16),
        name="reduce_route",
    )(owner, first, x)


def inverse_fourth_root(statistic, eye):
    matrix = statistic + RIDGE_TERM * eye
    scaling = 2.5 * lax.rsqrt(jnp.sum(matrix * matrix, keepdims=True))
    scaled = scaling * matrix
    factor = 1.25 * eye - 0.25 * scaled
    rounded = factor.astype(BF16)
    square = dot(rounded, rounded).astype(BF16)
    fourth = dot(square, square).astype(BF16)
    scaled = dot(fourth, scaled.astype(BF16))
    second = 1.25 * eye - 0.25 * scaled
    root = jnp.sqrt(jnp.sqrt(scaling))
    return root * dot(rounded, second.astype(BF16))


def block_kernel(
    refresh_ref, g_ref, r_ref, ls_ref, rs_ref, li_ref, ri_ref, upd_ref, la_ref, ra_ref, ln_ref, rn_ref
):
    grad = g_ref[:, 0].reshape(BLK, BLK)
    left_accum = DECAY_RATE * ls_ref[...] + (1.0 - DECAY_RATE) * dot_dims(grad, grad, NT)
    right_accum = DECAY_RATE * rs_ref[...] + (1.0 - DECAY_RATE) * dot_dims(grad, grad, TN)
    la_ref[...] = left_accum
    ra_ref[...] = right_accum

    left_root = r_ref[:, 0].reshape(BLK, BLK)
    right_root = r_ref[:, 1].reshape(BLK, BLK)
    high, low = split2(dot(left_root, g_ref[:, 1].reshape(BLK, BLK)))
    conditioned = dot(high, right_root) + dot(low, right_root)
    mean = jnp.sum(conditioned * conditioned, keepdims=True) * (1.0 / (BLK * BLK))
    upd_ref[...] = (conditioned * lax.rsqrt(mean + SCALE_EPSILON)).astype(BF16)

    @pl.when(refresh_ref[0, 0] > 0)
    def _():
        rows = lax.broadcasted_iota(jnp.int32, (BLK, BLK), 0)
        cols = lax.broadcasted_iota(jnp.int32, (BLK, BLK), 1)
        eye = (rows == cols).astype(F32)
        ln_ref[...] = inverse_fourth_root(la_ref[...], eye)
        rn_ref[...] = inverse_fourth_root(ra_ref[...], eye)

    @pl.when(refresh_ref[0, 0] <= 0)
    def _():
        ln_ref[...] = li_ref[...]
        rn_ref[...] = ri_ref[...]


def block_step(refresh, grads, roots, left_stats, right_stats, left_inverse, right_inverse):
    vmem = pl.BlockSpec(memory_space=pltpu.VMEM)
    square = jax.ShapeDtypeStruct((BLK, BLK), F32)
    return pl.pallas_call(
        block_kernel,
        in_specs=[pl.BlockSpec(memory_space=pltpu.SMEM)] + [vmem] * 6,
        out_specs=[vmem] * 5,
        out_shape=[jax.ShapeDtypeStruct((BLK, BLK), BF16)] + [square] * 4,
        compiler_params=pltpu.CompilerParams(vmem_limit_bytes=48 * 2**20),
        cost_estimate=pl.CostEstimate(flops=2**31, bytes_accessed=11 * 2**20, transcendentals=0),
        name="block_step",
    )(refresh, grads, roots, left_stats, right_stats, left_inverse, right_inverse)


def body(inputs, norm_gain, cotangent, owners, refresh, left_stats, right_stats, left_inverse, right_inverse):
    xl = lax.axis_index("xl").reshape(1)
    owner = owners[0]
    fsdp = lax.axis_size(FSDP)
    tokens, width = inputs.shape

    xt, squares = prepare(inputs, norm_gain)
    features = lax.all_gather(xt, ("z", "core"), axis=0, tiled=True)
    squares = jnp.broadcast_to(squares, (fsdp, tokens))
    squares, cotangent = lax.optimization_barrier((squares, cotangent))
    cot_other = lax.ppermute(cotangent, "xl", [(0, 1), (1, 0)])
    squares = lax.all_to_all(squares, FSDP, split_axis=0, concat_axis=0, tiled=True)
    squares = jnp.sum(squares, axis=0, keepdims=True)
    scale = lax.rsqrt(squares / (fsdp * width) + NORM_EPSILON)

    roots = stack_roots(left_inverse, right_inverse)
    roots, scale = lax.optimization_barrier((roots, scale))
    roots = lax.all_to_all(roots, GROUP, split_axis=0, concat_axis=0, tiled=True)
    roots = pick(roots, owner)
    roots = lax.all_to_all(roots, GROUP, split_axis=0, concat_axis=0, tiled=True)
    roots, features = lax.optimization_barrier((roots, features))

    halves = []
    for half in range(2):
        pieces = partials(xl, features, scale, cotangent, cot_other, half)
        pieces = pieces.reshape(2 * N_GROUP, 2, CHUNK, BLK)
        pieces = lax.all_to_all(pieces, ("y", "xh", "xl"), split_axis=0, concat_axis=0, tiled=True)
        halves.append(pieces.reshape(N_GROUP, 2, 2, CHUNK, BLK))
    grads = reduce_route(reduce_half(halves[0]), halves[1], owner)
    grads = lax.all_to_all(grads, GROUP, split_axis=0, concat_axis=0, tiled=True)
    return tuple(
        block_step(refresh, grads, roots, left_stats, right_stats, left_inverse, right_inverse)
    )


def solution(mesh):
    split = Mesh(mesh.devices.reshape(4, 2, 2, 8, 2), ("y", "xh", "xl", "z", "core"))
    both = P(GROUP, FSDP)
    in_specs = (both, P(FSDP), both, P(FSDP, None), both, both, both, both, both)
    return jax.shard_map(body, mesh=split, in_specs=in_specs, out_specs=(both,) * 5, check_vma=False)
```

```python
import jax
import jax.numpy as jnp
from jax import lax
from jax.experimental import pallas as pl
from jax.experimental.pallas import tpu as pltpu
from jax.sharding import Mesh
from jax.sharding import PartitionSpec as P

NORM_EPSILON = 1e-05
SCALE_EPSILON = 1e-06
DECAY_RATE = 0.95
RIDGE_TERM = 1e-06
BLK = 512
N_GROUP = 8
Z = 8
CHUNK = BLK // N_GROUP
WIDTH = 128
PER_SLAB = BLK // WIDTH
ROWS = WIDTH // N_GROUP
GROUP = ("y", "xh")
FSDP = ("xl", "z", "core")
SWAP = [(0, 1), (1, 0)]
BF16 = jnp.bfloat16
F32 = jnp.float32
NT = (((1,), (1,)), ((), ()))
TN = (((0,), (0,)), ((), ()))
EARLY = (0, -1, 1, -2, 2)
LATE = (-3, 3, 4)
HBM = pl.BlockSpec(memory_space=pltpu.HBM)
VMEM = pl.BlockSpec(memory_space=pltpu.VMEM)
SMEM = pl.BlockSpec(memory_space=pltpu.SMEM)


def in_hbm(x):
    return pltpu.with_memory_space_constraint(x, pltpu.HBM)


def params():
    return pltpu.CompilerParams(vmem_limit_bytes=48 * 2**20)


def dot(a, b):
    return jnp.dot(a, b, preferred_element_type=F32)


def dot_dims(a, b, dims):
    return lax.dot_general(a, b, dims, preferred_element_type=F32)


def split2(a):
    high = a.astype(BF16)
    return high, (a - high.astype(F32)).astype(BF16)


def prepare_kernel(x_ref, gain_ref, xt_ref, sq_ref):
    values = x_ref[...].astype(F32)
    xt_ref[...] = (values * gain_ref[...].astype(F32)).astype(BF16).T
    high, low = split2(values * values)
    ones = jnp.ones((8, values.shape[1]), BF16)
    sq_ref[...] = (dot_dims(ones, high, NT) + dot_dims(ones, low, NT))[:1]


def prepare(x, gain):
    tokens, width = x.shape
    step = tokens // 2
    return pl.pallas_call(
        prepare_kernel,
        grid=(2,),
        in_specs=[pl.BlockSpec((step, width), lambda i: (i, 0)), pl.BlockSpec((1, width), lambda i: (0, 0))],
        out_specs=[pl.BlockSpec((width, step), lambda i: (0, i)), pl.BlockSpec((1, step), lambda i: (0, i))],
        out_shape=[pltpu.HBM((width, tokens), BF16), jax.ShapeDtypeStruct((1, tokens), F32)],
        name="prepare",
    )(x, gain.reshape(1, width))


def stack_roots_kernel(l_ref, r_ref, o_ref):
    for i in range(N_GROUP):
        o_ref[i, 0] = l_ref[i * CHUNK : (i + 1) * CHUNK].astype(BF16)
        o_ref[i, 1] = r_ref[i * CHUNK : (i + 1) * CHUNK].astype(BF16)


def stack_roots(left, right):
    return pl.pallas_call(
        stack_roots_kernel,
        in_specs=[VMEM, VMEM],
        out_specs=VMEM,
        out_shape=pltpu.HBM((N_GROUP, 2, CHUNK, BLK), BF16),
        compiler_params=params(),
        name="stack_roots",
    )(left, right)


def partials_kernel(sizes, steps, *refs):
    count = len(sizes)
    xl_ref, scale_ref = refs[:2]
    x_refs = refs[2 : 2 + count]
    cot_refs = refs[2 + count : 4 + count]
    o_ref, x_buf, cot_buf, sems = refs[4 + count :]
    copies, start = [], 0
    for n, (x_ref, size) in enumerate(zip(x_refs, sizes)):
        copies.append(pltpu.make_async_copy(x_ref, x_buf.at[pl.ds(start, size)], sems.at[n]))
        start += size
    cot_copies = [pltpu.make_async_copy(cot_refs[n], cot_buf.at[n], sems.at[count + n]) for n in range(2)]
    cot_copies[0].start()
    for copy in copies:
        copy.start()
    cot_copies[1].start()
    span = start // steps
    for place in range(2):
        where = xl_ref[0] if place == 0 else 1 - xl_ref[0]
        for step in range(steps):
            if place == 0:
                if step == 0:
                    cot_copies[0].wait()
                taken = 0
                for n, size in enumerate(sizes):
                    if step * span <= taken < (step + 1) * span:
                        copies[n].wait()
                    taken += size
                rows = x_buf[step * span : (step + 1) * span].astype(F32) * scale_ref[...]
                x_buf[step * span : (step + 1) * span] = rows.astype(BF16)
            elif step == 0:
                cot_copies[1].wait()
            part = dot(x_buf[step * span : (step + 1) * span], cot_buf[place]).astype(BF16)
            for block in range(span // WIDTH):
                for g in range(N_GROUP):
                    first = block * WIDTH + g * ROWS
                    o_ref[g, where, step * (span // WIDTH) + block] = part[first : first + ROWS]


def partials(xl, scale, blocks, own, other, steps):
    sizes = tuple(b.shape[0] for b in blocks)
    rows, tokens = sum(sizes), own.shape[0]
    assert rows % (steps * WIDTH) == 0
    return pl.pallas_call(
        lambda *refs: partials_kernel(sizes, steps, *refs),
        in_specs=[SMEM, VMEM] + [HBM] * (len(sizes) + 2),
        out_specs=VMEM,
        out_shape=pltpu.HBM((N_GROUP, 2, rows // WIDTH, ROWS, BLK), BF16),
        scratch_shapes=[
            pltpu.VMEM((rows, tokens), BF16),
            pltpu.VMEM((2, tokens, BLK), BF16),
            pltpu.SemaphoreType.DMA((len(sizes) + 2,)),
        ],
        compiler_params=params(),
        cost_estimate=pl.CostEstimate(flops=4 * rows * tokens * BLK, bytes_accessed=10 * 2**20, transcendentals=0),
        name="partials",
    )(xl, scale, *[in_hbm(a) for a in (*blocks, own, other)])


def total(x_ref, block):
    acc = x_ref[0, 0, block].astype(F32)
    for g in range(1, N_GROUP):
        acc = acc + x_ref[g, 0, block].astype(F32)
    return acc.astype(BF16)


def reduce_kernel(x_ref, o_ref):
    for block in range(x_ref.shape[2]):
        o_ref[0, block] = total(x_ref, block)


def reduce_early(x):
    blocks = x.shape[2]
    return pl.pallas_call(
        reduce_kernel,
        grid=(2,),
        in_specs=[pl.BlockSpec((N_GROUP, 1, blocks, ROWS, BLK), lambda i: (0, i, 0, 0, 0))],
        out_specs=pl.BlockSpec((1, blocks, ROWS, BLK), lambda i: (i, 0, 0, 0)),
        out_shape=jax.ShapeDtypeStruct((2, blocks, ROWS, BLK), BF16),
        compiler_params=params(),
        name="reduce_early",
    )(x)


def route_kernel(owner_ref, place_ref, early_ref, roots_ref, x_ref, o_ref):
    half = pl.program_id(0)

    def put(offset, mate, value):
        z = lax.rem(place_ref[0] + offset + Z, Z)
        core = place_ref[1] if mate == 0 else 1 - place_ref[1]
        block = half * 2 * Z + z * 2 + core
        slab = block // PER_SLAB
        within = lax.rem(block, PER_SLAB)
        o_ref[slab, 1, within] = value
        o_ref[owner_ref[slab], 0, within] = value

    for n, offset in enumerate(EARLY):
        for mate in range(2):
            put(offset, mate, early_ref[0, 2 * n + mate])
    for i in range(N_GROUP // 2):
        dest = half * (N_GROUP // 2) + i
        o_ref[dest, 2] = roots_ref[owner_ref[dest], 0]
        o_ref[dest, 3] = roots_ref[owner_ref[dest], 1]
    for n, offset in enumerate(LATE):
        for mate in range(2):
            put(offset, mate, total(x_ref, 2 * n + mate))


def route(owner, place, early, roots, late):
    return pl.pallas_call(
        route_kernel,
        grid_spec=pltpu.PrefetchScalarGridSpec(
            num_scalar_prefetch=2,
            grid=(2,),
            in_specs=[
                pl.BlockSpec((1, *early.shape[1:]), lambda i, *s: (i, 0, 0, 0)),
                pl.BlockSpec(roots.shape, lambda i, *s: (0, 0, 0, 0, 0)),
                pl.BlockSpec((N_GROUP, 1, *late.shape[2:]), lambda i, *s: (0, i, 0, 0, 0)),
            ],
            out_specs=pl.BlockSpec((N_GROUP, 4, PER_SLAB, ROWS, BLK), lambda i, *s: (0, 0, 0, 0, 0)),
        ),
        out_shape=pltpu.HBM((N_GROUP, 4, PER_SLAB, ROWS, BLK), BF16),
        compiler_params=params(),
        name="route",
    )(owner, place, early, roots, late)


def inverse_fourth_root(statistic):
    rows = lax.broadcasted_iota(jnp.int32, (BLK, BLK), 0)
    cols = lax.broadcasted_iota(jnp.int32, (BLK, BLK), 1)
    eye = (rows == cols).astype(F32)
    matrix = statistic + RIDGE_TERM * eye
    scaling = 2.5 * lax.rsqrt(jnp.sum(matrix * matrix, keepdims=True))
    scaled = scaling * matrix
    factor = (1.25 * eye - 0.25 * scaled).astype(BF16)
    square = dot(factor, factor).astype(BF16)
    fourth = dot(square, square).astype(BF16)
    second = 1.25 * eye - 0.25 * dot(fourth, scaled.astype(BF16))
    return jnp.sqrt(jnp.sqrt(scaling)) * dot(factor, second.astype(BF16))


def block_kernel(
    refresh_ref, u_ref, ls_ref, rs_ref, li_ref, ri_ref, upd_ref, la_ref, ra_ref, ln_ref, rn_ref,
    left, right, left_new, right_new, grad, natural, sems,
):
    loads = [pltpu.make_async_copy(ls_ref, left, sems.at[0]), pltpu.make_async_copy(rs_ref, right, sems.at[1])]
    for load in loads:
        load.start()
    fresh = refresh_ref[0, 0] > 0
    keeps = [pltpu.make_async_copy(li_ref, ln_ref, sems.at[2]), pltpu.make_async_copy(ri_ref, rn_ref, sems.at[3])]

    @pl.when(jnp.logical_not(fresh))
    def _():
        for keep in keeps:
            keep.start()

    for i in range(PER_SLAB):
        for g in range(N_GROUP):
            first = i * WIDTH + g * ROWS
            grad[first : first + ROWS] = u_ref[g, 0, i]
            natural[first : first + ROWS] = u_ref[g, 1, i]

    stores = [pltpu.make_async_copy(left, la_ref, sems.at[4]), pltpu.make_async_copy(right, ra_ref, sems.at[5])]
    news = [pltpu.make_async_copy(left_new, ln_ref, sems.at[2]), pltpu.make_async_copy(right_new, rn_ref, sems.at[3])]
    for n, (accum, dims) in enumerate(((left, NT), (right, TN))):
        gram = dot_dims(grad[...], grad[...], dims)
        loads[n].wait()
        accum[...] = DECAY_RATE * accum[...] + (1.0 - DECAY_RATE) * gram
        stores[n].start()

    @pl.when(fresh)
    def _():
        for accum, new, copy in ((left, left_new, news[0]), (right, right_new, news[1])):
            new[...] = inverse_fourth_root(accum[...])
            copy.start()

    left_root = u_ref[:, 2].reshape(BLK, BLK)
    right_root = u_ref[:, 3].reshape(BLK, BLK)
    high, low = split2(dot(left_root, natural[...]))
    conditioned = dot(high, right_root) + dot(low, right_root)
    mean = jnp.sum(conditioned * conditioned, keepdims=True) * (1.0 / (BLK * BLK))
    upd_ref[...] = (conditioned * lax.rsqrt(mean + SCALE_EPSILON)).astype(BF16)

    for store in stores:
        store.wait()

    @pl.when(fresh)
    def _():
        for new in news:
            new.wait()

    @pl.when(jnp.logical_not(fresh))
    def _():
        for keep in keeps:
            keep.wait()


def block_step(refresh, received, left_stats, right_stats, left_inverse, right_inverse):
    square = pltpu.HBM((BLK, BLK), F32)
    return pl.pallas_call(
        block_kernel,
        in_specs=[SMEM, VMEM] + [HBM] * 4,
        out_specs=[VMEM] + [HBM] * 4,
        out_shape=[jax.ShapeDtypeStruct((BLK, BLK), BF16)] + [square] * 4,
        scratch_shapes=[pltpu.VMEM((BLK, BLK), F32)] * 4
        + [pltpu.VMEM((BLK, BLK), BF16)] * 2
        + [pltpu.SemaphoreType.DMA((6,))],
        compiler_params=params(),
        cost_estimate=pl.CostEstimate(flops=2**31, bytes_accessed=11 * 2**20, transcendentals=0),
        name="block_step",
    )(refresh, received, *[in_hbm(a) for a in (left_stats, right_stats, left_inverse, right_inverse)])


def shift(x, axis, by):
    size = lax.axis_size(axis)
    return lax.ppermute(x, axis, [(i, (i + by) % size) for i in range(size)])


def mate(x):
    return lax.ppermute(x, "core", SWAP)


def ring(block, squares):
    up = down = block
    order = [block, mate(block)]
    for step in range(3):
        up, down = shift(up, "z", 1), shift(down, "z", -1)
        if step == 0:
            up, down, squares = lax.optimization_barrier((up, down, squares))
        order += [up, mate(up), down, mate(down)]
    half = WIDTH // 2
    last = [shift(up[:half], "z", 1), shift(down[half:], "z", -1)]
    order += last + [mate(part) for part in last]
    return order[: 2 * len(EARLY)], order[2 * len(EARLY) :], squares


def body(inputs, norm_gain, cotangent, owners, refresh, left_stats, right_stats, left_inverse, right_inverse):
    xl, z, core = (lax.axis_index(name) for name in FSDP)
    owner = owners[0]
    tokens, width = inputs.shape
    features = lax.axis_size(FSDP) * width

    other = lax.ppermute(cotangent, "xl", SWAP)
    block, squares = prepare(inputs, norm_gain)

    peers = lax.axis_size(("z", "core"))
    squares = jnp.broadcast_to(squares, (peers, tokens))
    squares = lax.all_to_all(squares, ("z", "core"), split_axis=0, concat_axis=0, tiled=True)
    squares = jnp.sum(squares, axis=0, keepdims=True)
    early, late, squares = ring(block, squares)

    roots = stack_roots(left_inverse, right_inverse)
    roots, squares = lax.optimization_barrier((roots, squares))
    roots = lax.all_to_all(roots, GROUP, split_axis=0, concat_axis=0, tiled=True)
    early, late[0], late[2], squares = lax.optimization_barrier((early, late[0], late[2], squares))
    scale = lax.rsqrt((squares + lax.ppermute(squares, "xl", SWAP)) / features + NORM_EPSILON)

    received = []
    for blocks, steps in ((early, 2), (late, 1)):
        pieces = partials(xl.reshape(1), scale, blocks, cotangent, other, steps)
        shape = pieces.shape
        pieces = pieces.reshape(2 * N_GROUP, *shape[2:])
        pieces = lax.all_to_all(pieces, ("y", "xh", "xl"), split_axis=0, concat_axis=0, tiled=True)
        received.append(pieces.reshape(shape))
    roots = roots.reshape(N_GROUP, 2, PER_SLAB, ROWS, BLK)
    sent = route(owner, jnp.stack([z, core]), reduce_early(received[0]), roots, received[1])
    sent = lax.all_to_all(sent, GROUP, split_axis=0, concat_axis=0, tiled=True)
    return tuple(block_step(refresh, sent, left_stats, right_stats, left_inverse, right_inverse))


def solution(mesh):
    split = Mesh(mesh.devices.reshape(4, 2, 2, 8, 2), ("y", "xh", "xl", "z", "core"))
    both = P(GROUP, FSDP)
    in_specs = (both, P(FSDP), both, P(FSDP, None), both, both, both, both, both)
    return jax.shard_map(body, mesh=split, in_specs=in_specs, out_specs=(both,) * 5, check_vma=False)
```

```python
import jax
import jax.numpy as jnp
from jax import lax
from jax.experimental import pallas as pl
from jax.experimental.pallas import tpu as pltpu
from jax.sharding import Mesh
from jax.sharding import PartitionSpec as P

NORM_EPSILON = 1e-05
SCALE_EPSILON = 1e-06
DECAY_RATE = 0.95
RIDGE_TERM = 1e-06
BLK = 512
N_GROUP = 8
CHUNK = BLK // N_GROUP
PACKED = CHUNK + 16
GROUP = ("y", "xh")
FSDP = ("xl", "z", "core")
SWAP = [(0, 1), (1, 0)]
BF16 = jnp.bfloat16
F32 = jnp.float32
NT = (((1,), (1,)), ((), ()))
TN = (((0,), (0,)), ((), ()))
HBM = pl.BlockSpec(memory_space=pltpu.HBM)
VMEM = pl.BlockSpec(memory_space=pltpu.VMEM)
SMEM = pl.BlockSpec(memory_space=pltpu.SMEM)


def in_hbm(x):
    return pltpu.with_memory_space_constraint(x, pltpu.HBM)


def params():
    return pltpu.CompilerParams(vmem_limit_bytes=48 * 2**20)


def dot(a, b):
    return jnp.dot(a, b, preferred_element_type=F32)


def dot_dims(a, b, dims):
    return lax.dot_general(a, b, dims, preferred_element_type=F32)


def split2(a):
    high = a.astype(BF16)
    return high, (a - high.astype(F32)).astype(BF16)


def prepare_kernel(x_ref, gain_ref, xt_ref, sq_ref):
    values = x_ref[...].astype(F32)
    xt_ref[...] = (values * gain_ref[...].astype(F32)).astype(BF16).T
    high, low = split2(values * values)
    ones = jnp.ones((8, values.shape[1]), BF16)
    sq_ref[...] = (dot_dims(ones, high, NT) + dot_dims(ones, low, NT))[:1]


def prepare(x, gain):
    tokens, width = x.shape
    step = tokens // 2
    return pl.pallas_call(
        prepare_kernel,
        grid=(2,),
        in_specs=[pl.BlockSpec((step, width), lambda i: (i, 0)), pl.BlockSpec((1, width), lambda i: (0, 0))],
        out_specs=[pl.BlockSpec((width, step), lambda i: (0, i)), pl.BlockSpec((1, step), lambda i: (0, i))],
        out_shape=[pltpu.HBM((width, tokens), BF16), jax.ShapeDtypeStruct((1, tokens), F32)],
        name="prepare",
    )(x, gain.reshape(1, width))


def triangle():
    rows = lax.broadcasted_iota(jnp.int32, (BLK, BLK), 0)
    cols = lax.broadcasted_iota(jnp.int32, (BLK, BLK), 1)
    return rows, cols


def pack_roots_kernel(l_ref, r_ref, o_ref):
    rows, cols = triangle()
    left = l_ref[...]
    packed = jnp.where(cols > rows, left, r_ref[...]).astype(BF16)
    diagonal = jnp.sum(jnp.where(cols == rows, left, 0.0), axis=0, keepdims=True)
    diagonal = jnp.broadcast_to(diagonal, (PACKED - CHUNK, BLK)).astype(BF16)
    for i in range(N_GROUP):
        o_ref[i, :CHUNK] = packed[i * CHUNK : (i + 1) * CHUNK]
        o_ref[i, CHUNK:] = diagonal


def pack_roots(left, right):
    return pl.pallas_call(
        pack_roots_kernel,
        in_specs=[VMEM, VMEM],
        out_specs=VMEM,
        out_shape=pltpu.HBM((N_GROUP, PACKED, BLK), BF16),
        compiler_params=params(),
        name="pack_roots",
    )(left, right)


def pick_kernel(owner_ref, x_ref, o_ref):
    for i in range(N_GROUP):
        o_ref[i] = x_ref[owner_ref[i]]


def pick(owner, x):
    return pl.pallas_call(
        pick_kernel,
        in_specs=[SMEM, VMEM],
        out_specs=VMEM,
        out_shape=pltpu.HBM(x.shape, x.dtype),
        compiler_params=params(),
        name="pick",
    )(owner, x)


def unpack_roots_kernel(x_ref, l_ref, r_ref):
    rows, cols = triangle()
    packed = jnp.concatenate([x_ref[i, :CHUNK] for i in range(N_GROUP)], axis=0).astype(F32)
    upper = jnp.where(cols > rows, packed, 0.0)
    lower = jnp.where(cols < rows, packed, 0.0)
    diagonal = x_ref[0, CHUNK:].astype(F32)[:1]
    l_ref[...] = (upper + upper.T + jnp.where(cols == rows, diagonal, 0.0)).astype(BF16)
    r_ref[...] = (packed - upper + lower.T).astype(BF16)


def unpack_roots(x):
    square = jax.ShapeDtypeStruct((BLK, BLK), BF16)
    return pl.pallas_call(
        unpack_roots_kernel,
        in_specs=[VMEM],
        out_specs=[VMEM, VMEM],
        out_shape=[square, square],
        compiler_params=params(),
        name="unpack_roots",
    )(x)


def scale_kernel(scale_ref, x_ref, o_ref):
    column = jnp.broadcast_to(scale_ref[...], (8, scale_ref.shape[1])).T[:, :1]
    o_ref[...] = (x_ref[...].astype(F32) * column).astype(BF16)


def scaled(scale, x):
    tokens, cols = x.shape
    step = tokens // 4
    block = pl.BlockSpec((step, cols), lambda i: (i, 0))
    return pl.pallas_call(
        scale_kernel,
        grid=(4,),
        in_specs=[pl.BlockSpec((1, step), lambda i: (0, i)), block],
        out_specs=block,
        out_shape=jax.ShapeDtypeStruct(x.shape, BF16),
        name="scaled",
    )(scale, x)


def partial_kernel(xl_ref, x_ref, own_ref, other_ref, o_ref):
    for cot_ref, place in ((own_ref, xl_ref[0]), (other_ref, 1 - xl_ref[0])):
        part = dot(x_ref[...], cot_ref[...]).astype(BF16)
        for j in range(part.shape[0] // CHUNK):
            o_ref[j, place, 0] = part[j * CHUNK : (j + 1) * CHUNK]


def partials(xl, x, own, other, half):
    tokens = x.shape[1]
    whole = pl.BlockSpec((tokens, BLK), lambda i, xl: (0, 0))
    return pl.pallas_call(
        partial_kernel,
        grid_spec=pltpu.PrefetchScalarGridSpec(
            num_scalar_prefetch=1,
            grid=(4,),
            in_specs=[pl.BlockSpec((BLK // 2, tokens), lambda i, xl: (4 * half + i, 0)), whole, whole],
            out_specs=pl.BlockSpec((N_GROUP // 2, 2, 1, CHUNK, BLK), lambda i, xl: (i % 2, 0, i // 2, 0, 0)),
        ),
        out_shape=pltpu.HBM((N_GROUP, 2, 2, CHUNK, BLK), BF16),
        compiler_params=params(),
        cost_estimate=pl.CostEstimate(flops=8 * tokens * BLK * BLK, bytes_accessed=10 * 2**20, transcendentals=0),
        name="partials",
    )(xl, x, own, other)


def total(x_ref, slab):
    acc = x_ref[0, 0, slab].astype(F32)
    for g in range(1, N_GROUP):
        acc = acc + x_ref[g, 0, slab].astype(F32)
    return acc.astype(BF16)


def reduce_kernel(x_ref, o_ref):
    for slab in range(2):
        o_ref[0, slab] = total(x_ref, slab)


def reduce_half(x):
    return pl.pallas_call(
        reduce_kernel,
        grid=(2,),
        in_specs=[pl.BlockSpec((N_GROUP, 1, 2, CHUNK, BLK), lambda i: (0, i, 0, 0, 0))],
        out_specs=pl.BlockSpec((1, 2, CHUNK, BLK), lambda i: (i, 0, 0, 0)),
        out_shape=jax.ShapeDtypeStruct((2, 2, CHUNK, BLK), BF16),
        name="reduce_half",
    )(x)


def route_kernel(owner_ref, first_ref, x_ref, o_ref):
    base = 4 * pl.program_id(0)
    for n in range(2):
        for slab, value in ((base + n, first_ref[0, n]), (base + 2 + n, total(x_ref, n))):
            o_ref[slab, 1] = value
            o_ref[owner_ref[slab], 0] = value


def route(owner, first, x):
    return pl.pallas_call(
        route_kernel,
        grid_spec=pltpu.PrefetchScalarGridSpec(
            num_scalar_prefetch=1,
            grid=(2,),
            in_specs=[
                pl.BlockSpec((1, 2, CHUNK, BLK), lambda i, owner: (i, 0, 0, 0)),
                pl.BlockSpec((N_GROUP, 1, 2, CHUNK, BLK), lambda i, owner: (0, i, 0, 0, 0)),
            ],
            out_specs=pl.BlockSpec((N_GROUP, 2, CHUNK, BLK), lambda i, owner: (0, 0, 0, 0)),
        ),
        out_shape=pltpu.HBM((N_GROUP, 2, CHUNK, BLK), BF16),
        name="route",
    )(owner, first, in_hbm(x))


def inverse_fourth_root(statistic):
    rows, cols = triangle()
    eye = (rows == cols).astype(F32)
    matrix = statistic + RIDGE_TERM * eye
    scaling = 2.5 * lax.rsqrt(jnp.sum(matrix * matrix, keepdims=True))
    scaled = scaling * matrix
    factor = (1.25 * eye - 0.25 * scaled).astype(BF16)
    square = dot(factor, factor).astype(BF16)
    fourth = dot(square, square).astype(BF16)
    second = 1.25 * eye - 0.25 * dot(fourth, scaled.astype(BF16))
    return jnp.sqrt(jnp.sqrt(scaling)) * dot(factor, second.astype(BF16))


def block_kernel(
    refresh_ref, u_ref, lroot_ref, rroot_ref, ls_ref, rs_ref, li_ref, ri_ref,
    upd_ref, la_ref, ra_ref, ln_ref, rn_ref, left, right, left_new, right_new, sems,
):
    fresh = refresh_ref[0, 0] > 0
    loads = [pltpu.make_async_copy(ls_ref, left, sems.at[0]), pltpu.make_async_copy(rs_ref, right, sems.at[1])]
    keeps = [pltpu.make_async_copy(li_ref, left_new, sems.at[2]), pltpu.make_async_copy(ri_ref, right_new, sems.at[3])]
    stores = [pltpu.make_async_copy(left, la_ref, sems.at[4]), pltpu.make_async_copy(right, ra_ref, sems.at[5])]
    news = [pltpu.make_async_copy(left_new, ln_ref, sems.at[6]), pltpu.make_async_copy(right_new, rn_ref, sems.at[7])]
    for load in loads:
        load.start()

    @pl.when(jnp.logical_not(fresh))
    def _():
        for keep in keeps:
            keep.start()

    grad = u_ref[:, 0].reshape(BLK, BLK)
    for n, (accum, dims) in enumerate(((left, NT), (right, TN))):
        gram = dot_dims(grad, grad, dims)
        loads[n].wait()
        accum[...] = DECAY_RATE * accum[...] + (1.0 - DECAY_RATE) * gram
        stores[n].start()

    @pl.when(fresh)
    def _():
        for accum, new, copy in ((left, left_new, news[0]), (right, right_new, news[1])):
            new[...] = inverse_fourth_root(accum[...])
            copy.start()

    @pl.when(jnp.logical_not(fresh))
    def _():
        for keep, copy in zip(keeps, news):
            keep.wait()
            copy.start()

    right_root = rroot_ref[...]
    high, low = split2(dot(lroot_ref[...], u_ref[:, 1].reshape(BLK, BLK)))
    conditioned = dot(high, right_root) + dot(low, right_root)
    mean = jnp.sum(conditioned * conditioned, keepdims=True) * (1.0 / (BLK * BLK))
    upd_ref[...] = (conditioned * lax.rsqrt(mean + SCALE_EPSILON)).astype(BF16)
    for copy in stores + news:
        copy.wait()


def block_step(refresh, received, left_root, right_root, *state):
    square = pltpu.HBM((BLK, BLK), F32)
    return pl.pallas_call(
        block_kernel,
        in_specs=[SMEM, VMEM, VMEM, VMEM] + [HBM] * 4,
        out_specs=[VMEM] + [HBM] * 4,
        out_shape=[jax.ShapeDtypeStruct((BLK, BLK), BF16)] + [square] * 4,
        scratch_shapes=[pltpu.VMEM((BLK, BLK), F32)] * 4 + [pltpu.SemaphoreType.DMA((8,))],
        compiler_params=params(),
        cost_estimate=pl.CostEstimate(flops=2**31, bytes_accessed=11 * 2**20, transcendentals=0),
        name="block_step",
    )(refresh, received, left_root, right_root, *[in_hbm(a) for a in state])


def body(inputs, norm_gain, cotangent, owners, refresh, left_stats, right_stats, left_inverse, right_inverse):
    xl = lax.axis_index("xl").reshape(1)
    owner = owners[0]
    tokens, width = inputs.shape
    count = lax.axis_size(FSDP) * width
    peers = lax.axis_size(("z", "core"))

    block, squares = prepare(inputs, norm_gain)
    features = lax.all_gather(block, ("z", "core"), axis=0, tiled=True)
    squares_other = lax.ppermute(squares, "xl", SWAP)
    squares_other, cotangent = lax.optimization_barrier((squares_other, cotangent))
    other = lax.ppermute(cotangent, "xl", SWAP)

    roots = pack_roots(left_inverse, right_inverse)
    roots = lax.all_to_all(roots, GROUP, split_axis=0, concat_axis=0, tiled=True)
    squares = jnp.broadcast_to(squares + squares_other, (peers, tokens))
    roots, squares = lax.optimization_barrier((roots, squares))
    squares = lax.all_to_all(squares, ("z", "core"), split_axis=0, concat_axis=0, tiled=True)
    scale = lax.rsqrt(jnp.sum(squares, axis=0, keepdims=True) / count + NORM_EPSILON)
    roots = pick(owner, roots)
    roots, scale = lax.optimization_barrier((roots, scale))
    roots = lax.all_to_all(roots, GROUP, split_axis=0, concat_axis=0, tiled=True)
    own, other = scaled(scale, cotangent), scaled(scale, other)
    roots, features = lax.optimization_barrier((roots, features))

    halves = []
    for half in range(2):
        pieces = partials(xl, features, own, other, half)
        shape = pieces.shape
        pieces = pieces.reshape(2 * N_GROUP, *shape[2:])
        pieces = lax.all_to_all(pieces, ("y", "xh", "xl"), split_axis=0, concat_axis=0, tiled=True)
        halves.append(pieces.reshape(shape))
    grads = route(owner, reduce_half(halves[0]), halves[1])
    grads = lax.all_to_all(grads, GROUP, split_axis=0, concat_axis=0, tiled=True)
    left_root, right_root = unpack_roots(roots)
    state = (left_stats, right_stats, left_inverse, right_inverse)
    return tuple(block_step(refresh, grads, left_root, right_root, *state))


def solution(mesh):
    split = Mesh(mesh.devices.reshape(4, 2, 2, 8, 2), ("y", "xh", "xl", "z", "core"))
    both = P(GROUP, FSDP)
    in_specs = (both, P(FSDP), both, P(FSDP, None), both, both, both, both, both)
    return jax.shard_map(body, mesh=split, in_specs=in_specs, out_specs=(both,) * 5, check_vma=False)
```

```python
import jax
import jax.numpy as jnp
from jax import lax
from jax.experimental import pallas as pl
from jax.experimental.pallas import tpu as pltpu
from jax.sharding import Mesh
from jax.sharding import PartitionSpec as P

NORM_EPSILON = 1e-05
SCALE_EPSILON = 1e-06
DECAY_RATE = 0.95
RIDGE_TERM = 1e-06
BLK = 512
N_GROUP = 8
CHUNK = BLK // N_GROUP
PACKED = CHUNK + 16
GROUP = ("y", "xh")
FSDP = ("xl", "z", "core")
SWAP = [(0, 1), (1, 0)]
BF16 = jnp.bfloat16
F32 = jnp.float32
NT = (((1,), (1,)), ((), ()))
TN = (((0,), (0,)), ((), ()))
HBM = pl.BlockSpec(memory_space=pltpu.HBM)
VMEM = pl.BlockSpec(memory_space=pltpu.VMEM)
SMEM = pl.BlockSpec(memory_space=pltpu.SMEM)


def in_hbm(x):
    return pltpu.with_memory_space_constraint(x, pltpu.HBM)


def params():
    return pltpu.CompilerParams(vmem_limit_bytes=48 * 2**20)


def dot(a, b):
    return jnp.dot(a, b, preferred_element_type=F32)


def dot_dims(a, b, dims):
    return lax.dot_general(a, b, dims, preferred_element_type=F32)


def split2(a):
    high = a.astype(BF16)
    return high, (a - high.astype(F32)).astype(BF16)


def prepare_kernel(x_ref, gain_ref, xt_ref, sq_ref):
    values = x_ref[...].astype(F32)
    xt_ref[...] = (values * gain_ref[...].astype(F32)).astype(BF16).T
    high, low = split2(values * values)
    ones = jnp.ones((8, values.shape[1]), BF16)
    sq_ref[...] = (dot_dims(ones, high, NT) + dot_dims(ones, low, NT))[:1]


def prepare(x, gain):
    tokens, width = x.shape
    step = tokens // 2
    return pl.pallas_call(
        prepare_kernel,
        grid=(2,),
        in_specs=[pl.BlockSpec((step, width), lambda i: (i, 0)), pl.BlockSpec((1, width), lambda i: (0, 0))],
        out_specs=[pl.BlockSpec((width, step), lambda i: (0, i)), pl.BlockSpec((1, step), lambda i: (0, i))],
        out_shape=[pltpu.HBM((width, tokens), BF16), jax.ShapeDtypeStruct((1, tokens), F32)],
        name="prepare",
    )(x, gain.reshape(1, width))


def triangle():
    rows = lax.broadcasted_iota(jnp.int32, (BLK, BLK), 0)
    cols = lax.broadcasted_iota(jnp.int32, (BLK, BLK), 1)
    return rows, cols


def pack_roots_kernel(l_ref, r_ref, o_ref):
    rows, cols = triangle()
    left = l_ref[...]
    packed = jnp.where(cols > rows, left, r_ref[...]).astype(BF16)
    diagonal = jnp.sum(jnp.where(cols == rows, left, 0.0), axis=0, keepdims=True)
    diagonal = jnp.broadcast_to(diagonal, (PACKED - CHUNK, BLK)).astype(BF16)
    for i in range(N_GROUP):
        o_ref[i, :CHUNK] = packed[i * CHUNK : (i + 1) * CHUNK]
        o_ref[i, CHUNK:] = diagonal


def pack_roots(left, right):
    return pl.pallas_call(
        pack_roots_kernel,
        in_specs=[VMEM, VMEM],
        out_specs=VMEM,
        out_shape=pltpu.HBM((N_GROUP, PACKED, BLK), BF16),
        compiler_params=params(),
        name="pack_roots",
    )(left, right)


def pick_kernel(owner_ref, x_ref, o_ref):
    for i in range(N_GROUP):
        o_ref[i] = x_ref[owner_ref[i]]


def pick(owner, x):
    return pl.pallas_call(
        pick_kernel,
        in_specs=[SMEM, VMEM],
        out_specs=VMEM,
        out_shape=pltpu.HBM(x.shape, x.dtype),
        compiler_params=params(),
        name="pick",
    )(owner, x)


def unpack_roots_kernel(x_ref, l_ref, r_ref):
    rows, cols = triangle()
    packed = jnp.concatenate([x_ref[i, :CHUNK] for i in range(N_GROUP)], axis=0).astype(F32)
    upper = jnp.where(cols > rows, packed, 0.0)
    lower = jnp.where(cols < rows, packed, 0.0)
    diagonal = x_ref[0, CHUNK:].astype(F32)[:1]
    l_ref[...] = (upper + upper.T + jnp.where(cols == rows, diagonal, 0.0)).astype(BF16)
    r_ref[...] = (packed - upper + lower.T).astype(BF16)


def unpack_roots(x):
    square = jax.ShapeDtypeStruct((BLK, BLK), BF16)
    return pl.pallas_call(
        unpack_roots_kernel,
        in_specs=[VMEM],
        out_specs=[VMEM, VMEM],
        out_shape=[square, square],
        compiler_params=params(),
        name="unpack_roots",
    )(x)


def scale_kernel(scale_ref, x_ref, o_ref):
    column = jnp.broadcast_to(scale_ref[...], (8, scale_ref.shape[1])).T[:, :1]
    o_ref[...] = (x_ref[...].astype(F32) * column).astype(BF16)


def scaled(scale, x):
    tokens, cols = x.shape
    step = tokens // 4
    block = pl.BlockSpec((step, cols), lambda i: (i, 0))
    return pl.pallas_call(
        scale_kernel,
        grid=(4,),
        in_specs=[pl.BlockSpec((1, step), lambda i: (0, i)), block],
        out_specs=block,
        out_shape=jax.ShapeDtypeStruct(x.shape, BF16),
        name="scaled",
    )(scale, x)


def partial_kernel(xl_ref, x_ref, own_ref, other_ref, o_ref):
    for cot_ref, place in ((own_ref, xl_ref[0]), (other_ref, 1 - xl_ref[0])):
        part = dot(x_ref[...], cot_ref[...]).astype(BF16)
        for j in range(part.shape[0] // CHUNK):
            o_ref[j, place, 0] = part[j * CHUNK : (j + 1) * CHUNK]


def partials(xl, x, own, other):
    rows, tokens = x.shape
    slabs = rows // BLK
    return pl.pallas_call(
        partial_kernel,
        grid_spec=pltpu.PrefetchScalarGridSpec(
            num_scalar_prefetch=1,
            grid=(2 * slabs,),
            in_specs=[pl.BlockSpec((BLK // 2, tokens), lambda i, xl: (i, 0)), VMEM, VMEM],
            out_specs=pl.BlockSpec((N_GROUP // 2, 2, 1, CHUNK, BLK), lambda i, xl: (i % 2, 0, i // 2, 0, 0)),
        ),
        out_shape=pltpu.HBM((N_GROUP, 2, slabs, CHUNK, BLK), BF16),
        compiler_params=params(),
        cost_estimate=pl.CostEstimate(flops=4 * rows * tokens * BLK, bytes_accessed=16 * 2**20, transcendentals=0),
        name="partials",
    )(xl, x, own, other)


def total(x_ref, slab):
    acc = x_ref[0, 0, slab].astype(F32)
    for g in range(1, N_GROUP):
        acc = acc + x_ref[g, 0, slab].astype(F32)
    return acc.astype(BF16)


def route_kernel(owner_ref, x_ref, o_ref):
    base = 2 * pl.program_id(0)
    for n in range(2):
        value = total(x_ref, n)
        o_ref[base + n, 1] = value
        o_ref[owner_ref[base + n], 0] = value


def route(owner, x):
    return pl.pallas_call(
        route_kernel,
        grid_spec=pltpu.PrefetchScalarGridSpec(
            num_scalar_prefetch=1,
            grid=(4,),
            in_specs=[pl.BlockSpec((N_GROUP, 1, 2, CHUNK, BLK), lambda i, owner: (0, i // 2, i % 2, 0, 0))],
            out_specs=pl.BlockSpec((N_GROUP, 2, CHUNK, BLK), lambda i, owner: (0, 0, 0, 0)),
        ),
        out_shape=pltpu.HBM((N_GROUP, 2, CHUNK, BLK), BF16),
        compiler_params=params(),
        name="route",
    )(owner, x)


def inverse_fourth_root(statistic):
    rows, cols = triangle()
    eye = (rows == cols).astype(F32)
    matrix = statistic + RIDGE_TERM * eye
    scaling = 2.5 * lax.rsqrt(jnp.sum(matrix * matrix, keepdims=True))
    scaled = scaling * matrix
    factor = (1.25 * eye - 0.25 * scaled).astype(BF16)
    square = dot(factor, factor).astype(BF16)
    fourth = dot(square, square).astype(BF16)
    second = 1.25 * eye - 0.25 * dot(fourth, scaled.astype(BF16))
    return jnp.sqrt(jnp.sqrt(scaling)) * dot(factor, second.astype(BF16))


def block_kernel(
    refresh_ref, u_ref, lroot_ref, rroot_ref, ls_ref, rs_ref, li_ref, ri_ref,
    upd_ref, la_ref, ra_ref, ln_ref, rn_ref, left, right, left_new, right_new, sems,
):
    fresh = refresh_ref[0, 0] > 0
    loads = [pltpu.make_async_copy(ls_ref, left, sems.at[0]), pltpu.make_async_copy(rs_ref, right, sems.at[1])]
    keeps = [pltpu.make_async_copy(li_ref, left_new, sems.at[2]), pltpu.make_async_copy(ri_ref, right_new, sems.at[3])]
    stores = [pltpu.make_async_copy(left, la_ref, sems.at[4]), pltpu.make_async_copy(right, ra_ref, sems.at[5])]
    news = [pltpu.make_async_copy(left_new, ln_ref, sems.at[6]), pltpu.make_async_copy(right_new, rn_ref, sems.at[7])]
    for load in loads:
        load.start()

    @pl.when(jnp.logical_not(fresh))
    def _():
        for keep in keeps:
            keep.start()

    grad = u_ref[:, 0].reshape(BLK, BLK)
    for n, (accum, dims) in enumerate(((left, NT), (right, TN))):
        gram = dot_dims(grad, grad, dims)
        loads[n].wait()
        accum[...] = DECAY_RATE * accum[...] + (1.0 - DECAY_RATE) * gram
        stores[n].start()

    @pl.when(fresh)
    def _():
        for accum, new, copy in ((left, left_new, news[0]), (right, right_new, news[1])):
            new[...] = inverse_fourth_root(accum[...])
            copy.start()

    @pl.when(jnp.logical_not(fresh))
    def _():
        for keep, copy in zip(keeps, news):
            keep.wait()
            copy.start()

    right_root = rroot_ref[...]
    high, low = split2(dot(lroot_ref[...], u_ref[:, 1].reshape(BLK, BLK)))
    conditioned = dot(high, right_root) + dot(low, right_root)
    mean = jnp.sum(conditioned * conditioned, keepdims=True) * (1.0 / (BLK * BLK))
    upd_ref[...] = (conditioned * lax.rsqrt(mean + SCALE_EPSILON)).astype(BF16)
    for copy in stores + news:
        copy.wait()


def block_step(refresh, received, left_root, right_root, *state):
    square = pltpu.HBM((BLK, BLK), F32)
    return pl.pallas_call(
        block_kernel,
        in_specs=[SMEM, VMEM, VMEM, VMEM] + [HBM] * 4,
        out_specs=[VMEM] + [HBM] * 4,
        out_shape=[jax.ShapeDtypeStruct((BLK, BLK), BF16)] + [square] * 4,
        scratch_shapes=[pltpu.VMEM((BLK, BLK), F32)] * 4 + [pltpu.SemaphoreType.DMA((8,))],
        compiler_params=params(),
        cost_estimate=pl.CostEstimate(flops=2**31, bytes_accessed=11 * 2**20, transcendentals=0),
        name="block_step",
    )(refresh, received, left_root, right_root, *[in_hbm(a) for a in state])


def body(inputs, norm_gain, cotangent, owners, refresh, left_stats, right_stats, left_inverse, right_inverse):
    xl = lax.axis_index("xl").reshape(1)
    owner = owners[0]
    tokens, width = inputs.shape
    count = lax.axis_size(FSDP) * width
    peers = lax.axis_size(("z", "core"))

    other = lax.ppermute(cotangent, "xl", SWAP)
    block, squares = prepare(inputs, norm_gain)
    features = lax.all_gather(block, ("z", "core"), axis=0, tiled=True)
    squares = jnp.broadcast_to(squares, (peers, tokens))
    squares = lax.all_to_all(squares, ("z", "core"), split_axis=0, concat_axis=0, tiled=True)
    squares = jnp.sum(squares, axis=0, keepdims=True)

    roots = pack_roots(left_inverse, right_inverse)
    roots, squares = lax.optimization_barrier((roots, squares))
    scale = lax.rsqrt((squares + lax.ppermute(squares, "xl", SWAP)) / count + NORM_EPSILON)
    roots = lax.all_to_all(roots, GROUP, split_axis=0, concat_axis=0, tiled=True)
    roots = lax.all_to_all(pick(owner, roots), GROUP, split_axis=0, concat_axis=0, tiled=True)

    pieces = partials(xl, features, scaled(scale, cotangent), scaled(scale, other))
    shape = pieces.shape
    pieces, roots = lax.optimization_barrier((pieces.reshape(2 * N_GROUP, *shape[2:]), roots))
    pieces = lax.all_to_all(pieces, ("y", "xh", "xl"), split_axis=0, concat_axis=0, tiled=True)
    grads = route(owner, pieces.reshape(shape))
    grads = lax.all_to_all(grads, GROUP, split_axis=0, concat_axis=0, tiled=True)
    left_root, right_root = unpack_roots(roots)
    state = (left_stats, right_stats, left_inverse, right_inverse)
    return tuple(block_step(refresh, grads, left_root, right_root, *state))


def solution(mesh):
    split = Mesh(mesh.devices.reshape(4, 2, 2, 8, 2), ("y", "xh", "xl", "z", "core"))
    both = P(GROUP, FSDP)
    in_specs = (both, P(FSDP), both, P(FSDP, None), both, both, both, both, both)
    return jax.shard_map(body, mesh=split, in_specs=in_specs, out_specs=(both,) * 5, check_vma=False)
```

```python
import jax
import jax.numpy as jnp
from jax import lax
from jax.experimental import pallas as pl
from jax.experimental.pallas import tpu as pltpu
from jax.sharding import Mesh
from jax.sharding import PartitionSpec as P

NORM_EPSILON = 1e-05
SCALE_EPSILON = 1e-06
DECAY_RATE = 0.95
RIDGE_TERM = 1e-06
BLK = 512
N_GROUP = 8
CHUNK = BLK // N_GROUP
PACKED = CHUNK + 16
GROUP = ("y", "xh")
FSDP = ("xl", "z", "core")
SWAP = [(0, 1), (1, 0)]
BF16 = jnp.bfloat16
F32 = jnp.float32
NT = (((1,), (1,)), ((), ()))
TN = (((0,), (0,)), ((), ()))
HBM = pl.BlockSpec(memory_space=pltpu.HBM)
VMEM = pl.BlockSpec(memory_space=pltpu.VMEM)
SMEM = pl.BlockSpec(memory_space=pltpu.SMEM)


def in_hbm(x):
    return pltpu.with_memory_space_constraint(x, pltpu.HBM)


def params():
    return pltpu.CompilerParams(vmem_limit_bytes=48 * 2**20)


def dot(a, b):
    return jnp.dot(a, b, preferred_element_type=F32)


def dot_dims(a, b, dims):
    return lax.dot_general(a, b, dims, preferred_element_type=F32)


def split2(a):
    high = a.astype(BF16)
    return high, (a - high.astype(F32)).astype(BF16)


def prepare_kernel(x_ref, gain_ref, xt_ref, sq_ref):
    values = x_ref[...].astype(F32)
    xt_ref[...] = (values * gain_ref[...].astype(F32)).astype(BF16).T
    high, low = split2(values * values)
    ones = jnp.ones((8, values.shape[1]), BF16)
    sq_ref[...] = (dot_dims(ones, high, NT) + dot_dims(ones, low, NT))[:1]


def prepare(x, gain):
    tokens, width = x.shape
    step = tokens // 2
    return pl.pallas_call(
        prepare_kernel,
        grid=(2,),
        in_specs=[pl.BlockSpec((step, width), lambda i: (i, 0)), pl.BlockSpec((1, width), lambda i: (0, 0))],
        out_specs=[pl.BlockSpec((width, step), lambda i: (0, i)), pl.BlockSpec((1, step), lambda i: (0, i))],
        out_shape=[pltpu.HBM((width, tokens), BF16), jax.ShapeDtypeStruct((1, tokens), F32)],
        name="prepare",
    )(x, gain.reshape(1, width))


def triangle():
    rows = lax.broadcasted_iota(jnp.int32, (BLK, BLK), 0)
    cols = lax.broadcasted_iota(jnp.int32, (BLK, BLK), 1)
    return rows, cols


def pack_roots_kernel(l_ref, r_ref, o_ref):
    rows, cols = triangle()
    left = l_ref[...]
    packed = jnp.where(cols > rows, left, r_ref[...]).astype(BF16)
    diagonal = jnp.sum(jnp.where(cols == rows, left, 0.0), axis=0, keepdims=True)
    diagonal = jnp.broadcast_to(diagonal, (PACKED - CHUNK, BLK)).astype(BF16)
    for i in range(N_GROUP):
        o_ref[i, :CHUNK] = packed[i * CHUNK : (i + 1) * CHUNK]
        o_ref[i, CHUNK:] = diagonal


def pack_roots(left, right):
    return pl.pallas_call(
        pack_roots_kernel,
        in_specs=[VMEM, VMEM],
        out_specs=VMEM,
        out_shape=pltpu.HBM((N_GROUP, PACKED, BLK), BF16),
        compiler_params=params(),
        name="pack_roots",
    )(left, right)


def pick_kernel(owner_ref, x_ref, o_ref):
    for i in range(N_GROUP):
        o_ref[i] = x_ref[owner_ref[i]]


def pick(owner, x):
    return pl.pallas_call(
        pick_kernel,
        in_specs=[SMEM, VMEM],
        out_specs=VMEM,
        out_shape=pltpu.HBM(x.shape, x.dtype),
        compiler_params=params(),
        name="pick",
    )(owner, x)


def unpack_roots_kernel(x_ref, l_ref, r_ref):
    rows, cols = triangle()
    packed = jnp.concatenate([x_ref[i, :CHUNK] for i in range(N_GROUP)], axis=0).astype(F32)
    upper = jnp.where(cols > rows, packed, 0.0)
    lower = jnp.where(cols < rows, packed, 0.0)
    diagonal = x_ref[0, CHUNK:].astype(F32)[:1]
    l_ref[...] = (upper + upper.T + jnp.where(cols == rows, diagonal, 0.0)).astype(BF16)
    r_ref[...] = (packed - upper + lower.T).astype(BF16)


def unpack_roots(x):
    square = jax.ShapeDtypeStruct((BLK, BLK), BF16)
    return pl.pallas_call(
        unpack_roots_kernel,
        in_specs=[VMEM],
        out_specs=[VMEM, VMEM],
        out_shape=[square, square],
        compiler_params=params(),
        name="unpack_roots",
    )(x)


def partial_kernel(place_ref, x_ref, scale_ref, cot_ref, *refs):
    o_ref, scaled = refs[-2:]

    @pl.when(pl.program_id(0) == 0)
    def _():
        column = jnp.broadcast_to(scale_ref[...], (8, scale_ref.shape[1])).T[:, :1]
        scaled[...] = (cot_ref[...].astype(F32) * column).astype(BF16)

    part = dot(x_ref[...], scaled[...]).astype(BF16)
    for j in range(N_GROUP):
        o_ref[j, 0, 0] = part[j * CHUNK : (j + 1) * CHUNK]


def partials(place, x, scale, cot, *filled):
    rows, tokens = x.shape
    slabs = rows // BLK
    return pl.pallas_call(
        partial_kernel,
        grid_spec=pltpu.PrefetchScalarGridSpec(
            num_scalar_prefetch=1,
            grid=(slabs,),
            in_specs=[pl.BlockSpec((BLK, tokens), lambda i, place: (i, 0)), VMEM, VMEM] + [HBM] * len(filled),
            out_specs=pl.BlockSpec((N_GROUP, 1, 1, CHUNK, BLK), lambda i, place: (0, place[0], i, 0, 0)),
            scratch_shapes=[pltpu.VMEM((tokens, BLK), BF16)],
        ),
        out_shape=pltpu.HBM((N_GROUP, 2, slabs, CHUNK, BLK), BF16),
        input_output_aliases={4: 0} if filled else {},
        compiler_params=params(),
        cost_estimate=pl.CostEstimate(flops=2 * rows * tokens * BLK, bytes_accessed=12 * 2**20, transcendentals=0),
        name="partials",
    )(place, x, scale, cot, *filled)


def total(x_ref, slab):
    acc = x_ref[0, 0, slab].astype(F32)
    for g in range(1, N_GROUP):
        acc = acc + x_ref[g, 0, slab].astype(F32)
    return acc.astype(BF16)


def route_kernel(owner_ref, x_ref, o_ref):
    base = 2 * pl.program_id(0)
    for n in range(2):
        value = total(x_ref, n)
        o_ref[base + n, 1] = value
        o_ref[owner_ref[base + n], 0] = value


def route(owner, x):
    return pl.pallas_call(
        route_kernel,
        grid_spec=pltpu.PrefetchScalarGridSpec(
            num_scalar_prefetch=1,
            grid=(4,),
            in_specs=[pl.BlockSpec((N_GROUP, 1, 2, CHUNK, BLK), lambda i, owner: (0, i // 2, i % 2, 0, 0))],
            out_specs=pl.BlockSpec((N_GROUP, 2, CHUNK, BLK), lambda i, owner: (0, 0, 0, 0)),
        ),
        out_shape=pltpu.HBM((N_GROUP, 2, CHUNK, BLK), BF16),
        compiler_params=params(),
        name="route",
    )(owner, x)


def inverse_fourth_root(statistic):
    rows, cols = triangle()
    eye = (rows == cols).astype(F32)
    matrix = statistic + RIDGE_TERM * eye
    scaling = 2.5 * lax.rsqrt(jnp.sum(matrix * matrix, keepdims=True))
    scaled = scaling * matrix
    factor = (1.25 * eye - 0.25 * scaled).astype(BF16)
    square = dot(factor, factor).astype(BF16)
    fourth = dot(square, square).astype(BF16)
    second = 1.25 * eye - 0.25 * dot(fourth, scaled.astype(BF16))
    return jnp.sqrt(jnp.sqrt(scaling)) * dot(factor, second.astype(BF16))


def block_kernel(
    refresh_ref, u_ref, lroot_ref, rroot_ref, ls_ref, rs_ref, li_ref, ri_ref,
    upd_ref, la_ref, ra_ref, ln_ref, rn_ref, left, right, left_new, right_new, sems,
):
    fresh = refresh_ref[0, 0] > 0
    loads = [pltpu.make_async_copy(ls_ref, left, sems.at[0]), pltpu.make_async_copy(rs_ref, right, sems.at[1])]
    keeps = [pltpu.make_async_copy(li_ref, left_new, sems.at[2]), pltpu.make_async_copy(ri_ref, right_new, sems.at[3])]
    stores = [pltpu.make_async_copy(left, la_ref, sems.at[4]), pltpu.make_async_copy(right, ra_ref, sems.at[5])]
    news = [pltpu.make_async_copy(left_new, ln_ref, sems.at[6]), pltpu.make_async_copy(right_new, rn_ref, sems.at[7])]
    for load in loads:
        load.start()

    @pl.when(jnp.logical_not(fresh))
    def _():
        for keep in keeps:
            keep.start()

    grad = u_ref[:, 0].reshape(BLK, BLK)
    for n, (accum, dims) in enumerate(((left, NT), (right, TN))):
        gram = dot_dims(grad, grad, dims)
        loads[n].wait()
        accum[...] = DECAY_RATE * accum[...] + (1.0 - DECAY_RATE) * gram
        stores[n].start()

    @pl.when(fresh)
    def _():
        for accum, new, copy in ((left, left_new, news[0]), (right, right_new, news[1])):
            new[...] = inverse_fourth_root(accum[...])
            copy.start()

    @pl.when(jnp.logical_not(fresh))
    def _():
        for keep, copy in zip(keeps, news):
            keep.wait()
            copy.start()

    right_root = rroot_ref[...]
    high, low = split2(dot(lroot_ref[...], u_ref[:, 1].reshape(BLK, BLK)))
    conditioned = dot(high, right_root) + dot(low, right_root)
    mean = jnp.sum(conditioned * conditioned, keepdims=True) * (1.0 / (BLK * BLK))
    upd_ref[...] = (conditioned * lax.rsqrt(mean + SCALE_EPSILON)).astype(BF16)
    for copy in stores + news:
        copy.wait()


def block_step(refresh, received, left_root, right_root, *state):
    square = pltpu.HBM((BLK, BLK), F32)
    return pl.pallas_call(
        block_kernel,
        in_specs=[SMEM, VMEM, VMEM, VMEM] + [HBM] * 4,
        out_specs=[VMEM] + [HBM] * 4,
        out_shape=[jax.ShapeDtypeStruct((BLK, BLK), BF16)] + [square] * 4,
        scratch_shapes=[pltpu.VMEM((BLK, BLK), F32)] * 4 + [pltpu.SemaphoreType.DMA((8,))],
        compiler_params=params(),
        cost_estimate=pl.CostEstimate(flops=2**31, bytes_accessed=11 * 2**20, transcendentals=0),
        name="block_step",
    )(refresh, received, left_root, right_root, *[in_hbm(a) for a in state])


def body(inputs, norm_gain, cotangent, owners, refresh, left_stats, right_stats, left_inverse, right_inverse):
    xl = lax.axis_index("xl").reshape(1)
    owner = owners[0]
    tokens, width = inputs.shape
    count = lax.axis_size(FSDP) * width
    peers = lax.axis_size(("z", "core"))

    block, squares = prepare(inputs, norm_gain)
    features = lax.all_gather(block, ("z", "core"), axis=0, tiled=True)
    squares_other = lax.ppermute(squares, "xl", SWAP)
    roots = pack_roots(left_inverse, right_inverse)
    roots = lax.all_to_all(roots, GROUP, split_axis=0, concat_axis=0, tiled=True)
    roots, other, squares, squares_other = lax.optimization_barrier((roots, cotangent, squares, squares_other))
    other = lax.ppermute(other, "xl", SWAP)
    squares = jnp.broadcast_to(squares + squares_other, (peers, tokens))
    squares = lax.all_to_all(squares, ("z", "core"), split_axis=0, concat_axis=0, tiled=True)
    scale = lax.rsqrt(jnp.sum(squares, axis=0, keepdims=True) / count + NORM_EPSILON)
    roots = pick(owner, roots)
    roots, scale = lax.optimization_barrier((roots, scale))
    roots = lax.all_to_all(roots, GROUP, split_axis=0, concat_axis=0, tiled=True)

    pieces = partials(xl, features, scale, cotangent)
    pieces, other = lax.optimization_barrier((pieces, other))
    pieces = partials(1 - xl, features, scale, other, pieces)
    shape = pieces.shape
    pieces, roots = lax.optimization_barrier((pieces.reshape(2 * N_GROUP, *shape[2:]), roots))
    pieces = lax.all_to_all(pieces, ("y", "xh", "xl"), split_axis=0, concat_axis=0, tiled=True)
    grads = route(owner, pieces.reshape(shape))
    grads = lax.all_to_all(grads, GROUP, split_axis=0, concat_axis=0, tiled=True)
    left_root, right_root = unpack_roots(roots)
    state = (left_stats, right_stats, left_inverse, right_inverse)
    return tuple(block_step(refresh, grads, left_root, right_root, *state))


def solution(mesh):
    split = Mesh(mesh.devices.reshape(4, 2, 2, 8, 2), ("y", "xh", "xl", "z", "core"))
    both = P(GROUP, FSDP)
    in_specs = (both, P(FSDP), both, P(FSDP, None), both, both, both, both, both)
    return jax.shard_map(body, mesh=split, in_specs=in_specs, out_specs=(both,) * 5, check_vma=False)
```

```python
import jax
import jax.numpy as jnp
from jax import lax
from jax.experimental import pallas as pl
from jax.experimental.pallas import tpu as pltpu
from jax.sharding import Mesh
from jax.sharding import PartitionSpec as P

NORM_EPSILON = 1e-05
SCALE_EPSILON = 1e-06
DECAY_RATE = 0.95
RIDGE_TERM = 1e-06
BLK = 512
N_GROUP = 8
CHUNK = BLK // N_GROUP
PACKED = CHUNK + 16
GROUP = ("y", "xh")
FSDP = ("xl", "z", "core")
SWAP = [(0, 1), (1, 0)]
BF16 = jnp.bfloat16
F32 = jnp.float32
NT = (((1,), (1,)), ((), ()))
TN = (((0,), (0,)), ((), ()))
HBM = pl.BlockSpec(memory_space=pltpu.HBM)
VMEM = pl.BlockSpec(memory_space=pltpu.VMEM)
SMEM = pl.BlockSpec(memory_space=pltpu.SMEM)


def in_hbm(x):
    return pltpu.with_memory_space_constraint(x, pltpu.HBM)


def params():
    return pltpu.CompilerParams(vmem_limit_bytes=48 * 2**20)


def dot(a, b):
    return jnp.dot(a, b, preferred_element_type=F32)


def dot_dims(a, b, dims):
    return lax.dot_general(a, b, dims, preferred_element_type=F32)


def split2(a):
    high = a.astype(BF16)
    return high, (a - high.astype(F32)).astype(BF16)


def prepare_kernel(x_ref, gain_ref, xt_ref):
    xt_ref[...] = (x_ref[...].astype(F32) * gain_ref[...].astype(F32)).astype(BF16).T


def prepare(x, gain):
    tokens, width = x.shape
    step = tokens // 2
    return pl.pallas_call(
        prepare_kernel,
        grid=(2,),
        in_specs=[pl.BlockSpec((step, width), lambda i: (i, 0)), pl.BlockSpec((1, width), lambda i: (0, 0))],
        out_specs=pl.BlockSpec((width, step), lambda i: (0, i)),
        out_shape=pltpu.HBM((width, tokens), BF16),
        name="prepare",
    )(x, gain.reshape(1, width))


def triangle():
    rows = lax.broadcasted_iota(jnp.int32, (BLK, BLK), 0)
    cols = lax.broadcasted_iota(jnp.int32, (BLK, BLK), 1)
    return rows, cols


def pack_roots_kernel(l_ref, r_ref, o_ref, left, right, sems):
    copies = [pltpu.make_async_copy(l_ref, left, sems.at[0]), pltpu.make_async_copy(r_ref, right, sems.at[1])]
    for copy in copies:
        copy.start()
    for copy in copies:
        copy.wait()
    rows, cols = triangle()
    packed = jnp.where(cols > rows, left[...], right[...]).astype(BF16)
    diagonal = jnp.sum(jnp.where(cols == rows, left[...], 0.0), axis=0, keepdims=True)
    diagonal = jnp.broadcast_to(diagonal, (PACKED - CHUNK, BLK)).astype(BF16)
    for i in range(N_GROUP):
        o_ref[i, :CHUNK] = packed[i * CHUNK : (i + 1) * CHUNK]
        o_ref[i, CHUNK:] = diagonal


def pack_roots(left, right):
    return pl.pallas_call(
        pack_roots_kernel,
        in_specs=[HBM, HBM],
        out_specs=VMEM,
        out_shape=pltpu.HBM((N_GROUP, PACKED, BLK), BF16),
        scratch_shapes=[pltpu.VMEM((BLK, BLK), F32)] * 2 + [pltpu.SemaphoreType.DMA((2,))],
        compiler_params=params(),
        name="pack_roots",
    )(in_hbm(left), in_hbm(right))


def pick_kernel(owner_ref, x_ref, o_ref):
    for i in range(N_GROUP):
        o_ref[i] = x_ref[owner_ref[i]]


def pick(owner, x):
    return pl.pallas_call(
        pick_kernel,
        in_specs=[SMEM, VMEM],
        out_specs=VMEM,
        out_shape=pltpu.HBM(x.shape, x.dtype),
        compiler_params=params(),
        name="pick",
    )(owner, x)


def unpack_roots_kernel(x_ref, l_ref, r_ref):
    rows, cols = triangle()
    packed = jnp.concatenate([x_ref[i, :CHUNK] for i in range(N_GROUP)], axis=0).astype(F32)
    upper = jnp.where(cols > rows, packed, 0.0)
    lower = jnp.where(cols < rows, packed, 0.0)
    diagonal = x_ref[0, CHUNK:].astype(F32)[:1]
    l_ref[...] = (upper + upper.T + jnp.where(cols == rows, diagonal, 0.0)).astype(BF16)
    r_ref[...] = (packed - upper + lower.T).astype(BF16)


def unpack_roots(x):
    square = jax.ShapeDtypeStruct((BLK, BLK), BF16)
    return pl.pallas_call(
        unpack_roots_kernel,
        in_specs=[VMEM],
        out_specs=[VMEM, VMEM],
        out_shape=[square, square],
        compiler_params=params(),
        name="unpack_roots",
    )(x)


def column_of(scale_ref):
    return jnp.broadcast_to(scale_ref[...], (8, scale_ref.shape[1])).T[:, :1]


def scale_kernel(scale_ref, x_ref, o_ref):
    o_ref[...] = (x_ref[...].astype(F32) * column_of(scale_ref)).astype(BF16)


def scaled(scale, x):
    return pl.pallas_call(
        scale_kernel,
        in_specs=[VMEM, VMEM],
        out_specs=VMEM,
        out_shape=pltpu.HBM(x.shape, BF16),
        compiler_params=params(),
        name="scaled",
    )(scale, x)


def put_rows(o_ref, part):
    part = part.astype(BF16)
    for j in range(N_GROUP):
        o_ref[j, 0, 0] = part[j * CHUNK : (j + 1) * CHUNK]


def own_kernel(place_ref, x_ref, cot_ref, o_ref, local_ref, sems):
    @pl.when(pl.program_id(0) == 0)
    def _():
        spans = [pl.ds(first, BLK) for first in range(0, cot_ref.shape[0], BLK)]
        copies = [pltpu.make_async_copy(cot_ref.at[s], local_ref.at[s], sems.at[n]) for n, s in enumerate(spans)]
        for copy in copies:
            copy.start()
        part = jnp.zeros((BLK, BLK), F32)
        for copy, span in zip(copies, spans):
            copy.wait()
            part = part + dot(x_ref[:, span], local_ref[span])
        put_rows(o_ref, part)

    @pl.when(pl.program_id(0) > 0)
    def _():
        put_rows(o_ref, dot(x_ref[...], local_ref[...]))


def other_kernel(place_ref, x_ref, cot_ref, scale_ref, filled_ref, o_ref, scaled_ref):
    @pl.when(pl.program_id(0) == 0)
    def _():
        column = column_of(scale_ref)
        part = jnp.zeros((BLK, BLK), F32)
        for first in range(0, cot_ref.shape[0], BLK):
            span = slice(first, first + BLK)
            piece = (cot_ref[span].astype(F32) * column[span]).astype(BF16)
            scaled_ref[span] = piece
            part = part + dot(x_ref[:, span], piece)
        put_rows(o_ref, part)

    @pl.when(pl.program_id(0) > 0)
    def _():
        put_rows(o_ref, dot(x_ref[...], scaled_ref[...]))


def partials(place, x, cot, *rest):
    rows, tokens = x.shape
    slabs = rows // BLK
    return pl.pallas_call(
        other_kernel if rest else own_kernel,
        grid_spec=pltpu.PrefetchScalarGridSpec(
            num_scalar_prefetch=1,
            grid=(slabs,),
            in_specs=[pl.BlockSpec((BLK, tokens), lambda i, place: (i, 0))] + ([VMEM, VMEM, HBM] if rest else [HBM]),
            out_specs=pl.BlockSpec((N_GROUP, 1, 1, CHUNK, BLK), lambda i, place: (0, place[0], i, 0, 0)),
            scratch_shapes=[pltpu.VMEM((tokens, BLK), BF16)]
            + ([] if rest else [pltpu.SemaphoreType.DMA((tokens // BLK,))]),
        ),
        out_shape=pltpu.HBM((N_GROUP, 2, slabs, CHUNK, BLK), BF16),
        input_output_aliases={4: 0} if rest else {},
        compiler_params=params(),
        cost_estimate=pl.CostEstimate(flops=2 * rows * tokens * BLK, bytes_accessed=12 * 2**20, transcendentals=0),
        name="partials",
    )(place, x, cot if rest else in_hbm(cot), *rest)


def total(x_ref, slab):
    acc = x_ref[0, 0, slab].astype(F32)
    for g in range(1, N_GROUP):
        acc = acc + x_ref[g, 0, slab].astype(F32)
    return acc.astype(BF16)


def route_kernel(owner_ref, x_ref, o_ref):
    base = 2 * pl.program_id(0)
    for n in range(2):
        value = total(x_ref, n)
        o_ref[base + n, 1] = value
        o_ref[owner_ref[base + n], 0] = value


def route(owner, x):
    return pl.pallas_call(
        route_kernel,
        grid_spec=pltpu.PrefetchScalarGridSpec(
            num_scalar_prefetch=1,
            grid=(4,),
            in_specs=[pl.BlockSpec((N_GROUP, 1, 2, CHUNK, BLK), lambda i, owner: (0, i // 2, i % 2, 0, 0))],
            out_specs=pl.BlockSpec((N_GROUP, 2, CHUNK, BLK), lambda i, owner: (0, 0, 0, 0)),
        ),
        out_shape=pltpu.HBM((N_GROUP, 2, CHUNK, BLK), BF16),
        compiler_params=params(),
        name="route",
    )(owner, x)


def inverse_fourth_root(statistic):
    rows, cols = triangle()
    eye = (rows == cols).astype(F32)
    matrix = statistic + RIDGE_TERM * eye
    scaling = 2.5 * lax.rsqrt(jnp.sum(matrix * matrix, keepdims=True))
    scaled = scaling * matrix
    factor = (1.25 * eye - 0.25 * scaled).astype(BF16)
    square = dot(factor, factor).astype(BF16)
    fourth = dot(square, square).astype(BF16)
    second = 1.25 * eye - 0.25 * dot(fourth, scaled.astype(BF16))
    return jnp.sqrt(jnp.sqrt(scaling)) * dot(factor, second.astype(BF16))


def block_kernel(
    refresh_ref, u_ref, lroot_ref, rroot_ref, ls_ref, rs_ref, li_ref, ri_ref,
    upd_ref, la_ref, ra_ref, ln_ref, rn_ref, left, right, left_new, right_new, sems,
):
    fresh = refresh_ref[0, 0] > 0
    loads = [pltpu.make_async_copy(ls_ref, left, sems.at[0]), pltpu.make_async_copy(rs_ref, right, sems.at[1])]
    keeps = [pltpu.make_async_copy(li_ref, left_new, sems.at[2]), pltpu.make_async_copy(ri_ref, right_new, sems.at[3])]
    stores = [pltpu.make_async_copy(left, la_ref, sems.at[4]), pltpu.make_async_copy(right, ra_ref, sems.at[5])]
    news = [pltpu.make_async_copy(left_new, ln_ref, sems.at[6]), pltpu.make_async_copy(right_new, rn_ref, sems.at[7])]
    for load in loads:
        load.start()

    @pl.when(jnp.logical_not(fresh))
    def _():
        for keep in keeps:
            keep.start()

    grad = u_ref[:, 0].reshape(BLK, BLK)
    for n, (accum, dims) in enumerate(((left, NT), (right, TN))):
        gram = dot_dims(grad, grad, dims)
        loads[n].wait()
        accum[...] = DECAY_RATE * accum[...] + (1.0 - DECAY_RATE) * gram
        stores[n].start()

    @pl.when(fresh)
    def _():
        for accum, new, copy in ((left, left_new, news[0]), (right, right_new, news[1])):
            new[...] = inverse_fourth_root(accum[...])
            copy.start()

    @pl.when(jnp.logical_not(fresh))
    def _():
        for keep, copy in zip(keeps, news):
            keep.wait()
            copy.start()

    right_root = rroot_ref[...]
    high, low = split2(dot(lroot_ref[...], u_ref[:, 1].reshape(BLK, BLK)))
    conditioned = dot(high, right_root) + dot(low, right_root)
    mean = jnp.sum(conditioned * conditioned, keepdims=True) * (1.0 / (BLK * BLK))
    upd_ref[...] = (conditioned * lax.rsqrt(mean + SCALE_EPSILON)).astype(BF16)
    for copy in stores + news:
        copy.wait()


def block_step(refresh, received, left_root, right_root, *state):
    square = pltpu.HBM((BLK, BLK), F32)
    return pl.pallas_call(
        block_kernel,
        in_specs=[SMEM, VMEM, VMEM, VMEM] + [HBM] * 4,
        out_specs=[VMEM] + [HBM] * 4,
        out_shape=[jax.ShapeDtypeStruct((BLK, BLK), BF16)] + [square] * 4,
        scratch_shapes=[pltpu.VMEM((BLK, BLK), F32)] * 4 + [pltpu.SemaphoreType.DMA((8,))],
        compiler_params=params(),
        cost_estimate=pl.CostEstimate(flops=2**31, bytes_accessed=11 * 2**20, transcendentals=0),
        name="block_step",
    )(refresh, received, left_root, right_root, *[in_hbm(a) for a in state])


def body(inputs, norm_gain, cotangent, owners, refresh, left_stats, right_stats, left_inverse, right_inverse):
    xl = lax.axis_index("xl").reshape(1)
    owner = owners[0]
    tokens, width = inputs.shape
    count = lax.axis_size(FSDP) * width
    peers = lax.axis_size(("z", "core"))

    features = lax.all_gather(prepare(inputs, norm_gain), ("z", "core"), axis=0, tiled=True)
    values = inputs.astype(F32)
    squares = jnp.sum(values * values, axis=1).reshape(1, tokens)
    roots = pack_roots(left_inverse, right_inverse)
    squares_other = lax.ppermute(squares, "xl", SWAP)
    roots = lax.all_to_all(roots, GROUP, split_axis=0, concat_axis=0, tiled=True)
    roots, other, squares, squares_other = lax.optimization_barrier((roots, cotangent, squares, squares_other))
    other = lax.ppermute(other, "xl", SWAP)
    squares = jnp.broadcast_to(squares + squares_other, (peers, tokens))
    squares = lax.all_to_all(squares, ("z", "core"), split_axis=0, concat_axis=0, tiled=True)
    scale = lax.rsqrt(jnp.sum(squares, axis=0, keepdims=True) / count + NORM_EPSILON)
    roots = pick(owner, roots)
    roots, scale = lax.optimization_barrier((roots, scale))
    roots = lax.all_to_all(roots, GROUP, split_axis=0, concat_axis=0, tiled=True)

    pieces = partials(xl, features, scaled(scale, cotangent))
    pieces, other = lax.optimization_barrier((pieces, other))
    pieces = partials(1 - xl, features, other, scale, pieces)
    shape = pieces.shape
    pieces, roots = lax.optimization_barrier((pieces.reshape(2 * N_GROUP, *shape[2:]), roots))
    pieces = lax.all_to_all(pieces, ("y", "xh", "xl"), split_axis=0, concat_axis=0, tiled=True)
    grads = route(owner, pieces.reshape(shape))
    grads = lax.all_to_all(grads, GROUP, split_axis=0, concat_axis=0, tiled=True)
    left_root, right_root = unpack_roots(roots)
    state = (left_stats, right_stats, left_inverse, right_inverse)
    return tuple(block_step(refresh, grads, left_root, right_root, *state))


def solution(mesh):
    split = Mesh(mesh.devices.reshape(4, 2, 2, 8, 2), ("y", "xh", "xl", "z", "core"))
    both = P(GROUP, FSDP)
    in_specs = (both, P(FSDP), both, P(FSDP, None), both, both, both, both, both)
    return jax.shard_map(body, mesh=split, in_specs=in_specs, out_specs=(both,) * 5, check_vma=False)
```

```python
import jax
import jax.numpy as jnp
from jax import lax
from jax.experimental import pallas as pl
from jax.experimental.pallas import tpu as pltpu
from jax.sharding import Mesh
from jax.sharding import PartitionSpec as P

NORM_EPSILON = 1e-05
SCALE_EPSILON = 1e-06
DECAY_RATE = 0.95
RIDGE_TERM = 1e-06
BLK = 512
N_GROUP = 8
LOAD = 512
CHUNK = BLK // N_GROUP
PACKED = CHUNK + 16
GROUP = ("y", "xh")
FSDP = ("xl", "z", "core")
SWAP = [(0, 1), (1, 0)]
BF16 = jnp.bfloat16
F32 = jnp.float32
NT = (((1,), (1,)), ((), ()))
TN = (((0,), (0,)), ((), ()))
HBM = pl.BlockSpec(memory_space=pltpu.HBM)
VMEM = pl.BlockSpec(memory_space=pltpu.VMEM)
SMEM = pl.BlockSpec(memory_space=pltpu.SMEM)


def in_hbm(x):
    return pltpu.with_memory_space_constraint(x, pltpu.HBM)


def params():
    return pltpu.CompilerParams(vmem_limit_bytes=48 * 2**20)


def dot(a, b):
    return jnp.dot(a, b, preferred_element_type=F32)


def dot_dims(a, b, dims):
    return lax.dot_general(a, b, dims, preferred_element_type=F32)


def split2(a):
    high = a.astype(BF16)
    return high, (a - high.astype(F32)).astype(BF16)


def prepare_kernel(x_ref, gain_ref, xt_ref):
    xt_ref[...] = (x_ref[...].astype(F32) * gain_ref[...].astype(F32)).astype(BF16).T


def prepare(x, gain):
    tokens, width = x.shape
    step = tokens // 2
    return pl.pallas_call(
        prepare_kernel,
        grid=(2,),
        in_specs=[pl.BlockSpec((step, width), lambda i: (i, 0)), pl.BlockSpec((1, width), lambda i: (0, 0))],
        out_specs=pl.BlockSpec((width, step), lambda i: (0, i)),
        out_shape=pltpu.HBM((width, tokens), BF16),
        name="prepare",
    )(x, gain.reshape(1, width))


def triangle():
    rows = lax.broadcasted_iota(jnp.int32, (BLK, BLK), 0)
    cols = lax.broadcasted_iota(jnp.int32, (BLK, BLK), 1)
    return rows, cols


def pack_roots_kernel(l_ref, r_ref, o_ref, left, right, sems):
    copies = [pltpu.make_async_copy(l_ref, left, sems.at[0]), pltpu.make_async_copy(r_ref, right, sems.at[1])]
    for copy in copies:
        copy.start()
    for copy in copies:
        copy.wait()
    rows, cols = triangle()
    packed = jnp.where(cols > rows, left[...], right[...]).astype(BF16)
    diagonal = jnp.sum(jnp.where(cols == rows, left[...], 0.0), axis=0, keepdims=True)
    diagonal = jnp.broadcast_to(diagonal, (PACKED - CHUNK, BLK)).astype(BF16)
    for i in range(N_GROUP):
        o_ref[i, :CHUNK] = packed[i * CHUNK : (i + 1) * CHUNK]
        o_ref[i, CHUNK:] = diagonal


def pack_roots(left, right):
    return pl.pallas_call(
        pack_roots_kernel,
        in_specs=[HBM, HBM],
        out_specs=VMEM,
        out_shape=pltpu.HBM((N_GROUP, PACKED, BLK), BF16),
        scratch_shapes=[pltpu.VMEM((BLK, BLK), F32)] * 2 + [pltpu.SemaphoreType.DMA((2,))],
        compiler_params=params(),
        name="pack_roots",
    )(in_hbm(left), in_hbm(right))


def pick_kernel(owner_ref, x_ref, o_ref):
    for i in range(N_GROUP):
        o_ref[i] = x_ref[owner_ref[i]]


def pick(owner, x):
    return pl.pallas_call(
        pick_kernel,
        in_specs=[SMEM, VMEM],
        out_specs=VMEM,
        out_shape=pltpu.HBM(x.shape, x.dtype),
        compiler_params=params(),
        name="pick",
    )(owner, x)


def unpack_roots_kernel(x_ref, l_ref, r_ref):
    rows, cols = triangle()
    packed = jnp.concatenate([x_ref[i, :CHUNK] for i in range(N_GROUP)], axis=0).astype(F32)
    upper = jnp.where(cols > rows, packed, 0.0)
    lower = jnp.where(cols < rows, packed, 0.0)
    diagonal = x_ref[0, CHUNK:].astype(F32)[:1]
    l_ref[...] = (upper + upper.T + jnp.where(cols == rows, diagonal, 0.0)).astype(BF16)
    r_ref[...] = (packed - upper + lower.T).astype(BF16)


def unpack_roots(x):
    square = jax.ShapeDtypeStruct((BLK, BLK), BF16)
    return pl.pallas_call(
        unpack_roots_kernel,
        in_specs=[VMEM],
        out_specs=[VMEM, VMEM],
        out_shape=[square, square],
        compiler_params=params(),
        name="unpack_roots",
    )(x)


def column_of(scale_ref):
    return jnp.broadcast_to(scale_ref[...], (8, scale_ref.shape[1])).T[:, :1]


def scale_kernel(scale_ref, x_ref, o_ref):
    o_ref[...] = (x_ref[...].astype(F32) * column_of(scale_ref)).astype(BF16)


def scaled(scale, x):
    return pl.pallas_call(
        scale_kernel,
        in_specs=[VMEM, VMEM],
        out_specs=VMEM,
        out_shape=pltpu.HBM(x.shape, BF16),
        compiler_params=params(),
        name="scaled",
    )(scale, x)


def partials_kernel(place_ref, x_ref, cot_ref, *refs):
    *rest, o_ref, local, scaled_ref, part_ref, sems = refs
    rows, tokens = local.shape
    slabs, pieces = rows // BLK, rows // LOAD
    loads = [
        pltpu.make_async_copy(x_ref.at[pl.ds(n * LOAD, LOAD)], local.at[pl.ds(n * LOAD, LOAD)], sems.at[n])
        for n in range(pieces)
    ]
    spans = [pl.ds(first, BLK) for first in range(0, tokens, BLK)]
    cots = [
        pltpu.make_async_copy(cot_ref.at[span], scaled_ref.at[span], sems.at[pieces + n])
        for n, span in enumerate(spans)
    ]
    stores = [
        pltpu.make_async_copy(part_ref.at[i], o_ref.at[:, place_ref[0], i], sems.at[pieces + len(spans) + i])
        for i in range(slabs)
    ]
    for load in loads[: BLK // LOAD]:
        load.start()
    if not rest:
        for copy in cots:
            copy.start()
    for load in loads[BLK // LOAD :]:
        load.start()
    if rest:
        column = column_of(rest[0])
        for span in spans:
            scaled_ref[span] = (cot_ref[span].astype(F32) * column[span.start : span.start + BLK]).astype(BF16)
    else:
        for copy in cots:
            copy.wait()
    for i in range(slabs):
        for load in loads[i * (BLK // LOAD) : (i + 1) * (BLK // LOAD)]:
            load.wait()
        part = dot(local[i * BLK : (i + 1) * BLK], scaled_ref[...]).astype(BF16)
        for j in range(N_GROUP):
            part_ref[i, j] = part[j * CHUNK : (j + 1) * CHUNK]
        stores[i].start()
    for store in stores:
        store.wait()


def partials(place, x, cot, *rest):
    rows, tokens = x.shape
    slabs = rows // BLK
    return pl.pallas_call(
        partials_kernel,
        in_specs=[SMEM, HBM] + ([VMEM, VMEM, HBM] if rest else [HBM]),
        out_specs=HBM,
        scratch_shapes=[
            pltpu.VMEM((rows, tokens), BF16),
            pltpu.VMEM((tokens, BLK), BF16),
            pltpu.VMEM((slabs, N_GROUP, CHUNK, BLK), BF16),
            pltpu.SemaphoreType.DMA((rows // LOAD + tokens // BLK + slabs,)),
        ],
        out_shape=pltpu.HBM((N_GROUP, 2, slabs, CHUNK, BLK), BF16),
        input_output_aliases={4: 0} if rest else {},
        compiler_params=params(),
        cost_estimate=pl.CostEstimate(flops=2 * rows * tokens * BLK, bytes_accessed=12 * 2**20, transcendentals=0),
        name="partials",
    )(place, in_hbm(x), cot if rest else in_hbm(cot), *rest)


def route_kernel(owner_ref, x_ref, o_ref):
    for half in range(2):
        for n in range(x_ref.shape[2]):
            value = x_ref[0, half, n].astype(F32)
            for g in range(1, N_GROUP):
                value = value + x_ref[g, half, n].astype(F32)
            value = value.astype(BF16)
            slab = half * x_ref.shape[2] + n
            o_ref[slab, 1] = value
            o_ref[owner_ref[slab], 0] = value


def route(owner, x):
    return pl.pallas_call(
        route_kernel,
        in_specs=[SMEM, VMEM],
        out_specs=VMEM,
        out_shape=pltpu.HBM((N_GROUP, 2, CHUNK, BLK), BF16),
        compiler_params=params(),
        name="route",
    )(owner, x)


def inverse_fourth_root(statistic):
    rows, cols = triangle()
    eye = (rows == cols).astype(F32)
    matrix = statistic + RIDGE_TERM * eye
    scaling = 2.5 * lax.rsqrt(jnp.sum(matrix * matrix, keepdims=True))
    matrix = scaling * matrix
    rounded = matrix.astype(BF16)
    product = dot(rounded, rounded)
    square = (1.5625 * eye - 0.625 * matrix + 0.0625 * product).astype(BF16)
    once = (1.25 * matrix - 0.25 * product).astype(BF16)
    fourth = dot(square, square).astype(BF16)
    return jnp.sqrt(jnp.sqrt(scaling)) * (1.5625 * eye - 0.3125 * matrix - 0.25 * dot(fourth, once))


def block_kernel(
    refresh_ref, u_ref, lroot_ref, rroot_ref, ls_ref, rs_ref, li_ref, ri_ref,
    upd_ref, la_ref, ra_ref, ln_ref, rn_ref, left, right, left_new, right_new, sems,
):
    fresh = refresh_ref[0, 0] > 0
    loads = [pltpu.make_async_copy(ls_ref, left, sems.at[0]), pltpu.make_async_copy(rs_ref, right, sems.at[1])]
    keeps = [pltpu.make_async_copy(li_ref, left_new, sems.at[2]), pltpu.make_async_copy(ri_ref, right_new, sems.at[3])]
    stores = [pltpu.make_async_copy(left, la_ref, sems.at[4]), pltpu.make_async_copy(right, ra_ref, sems.at[5])]
    news = [pltpu.make_async_copy(left_new, ln_ref, sems.at[6]), pltpu.make_async_copy(right_new, rn_ref, sems.at[7])]
    for load in loads:
        load.start()

    @pl.when(jnp.logical_not(fresh))
    def _():
        for keep in keeps:
            keep.start()

    grad = u_ref[:, 0].reshape(BLK, BLK)
    for n, (accum, dims) in enumerate(((left, NT), (right, TN))):
        gram = dot_dims(grad, grad, dims)
        loads[n].wait()
        accum[...] = DECAY_RATE * accum[...] + (1.0 - DECAY_RATE) * gram
        stores[n].start()

    @pl.when(fresh)
    def _():
        for accum, new, copy in ((left, left_new, news[0]), (right, right_new, news[1])):
            new[...] = inverse_fourth_root(accum[...])
            copy.start()

    @pl.when(jnp.logical_not(fresh))
    def _():
        for keep, copy in zip(keeps, news):
            keep.wait()
            copy.start()

    right_root = rroot_ref[...]
    high, low = split2(dot(lroot_ref[...], u_ref[:, 1].reshape(BLK, BLK)))
    conditioned = dot(high, right_root) + dot(low, right_root)
    mean = jnp.sum(conditioned * conditioned, keepdims=True) * (1.0 / (BLK * BLK))
    upd_ref[...] = (conditioned * lax.rsqrt(mean + SCALE_EPSILON)).astype(BF16)
    for copy in stores + news:
        copy.wait()


def block_step(refresh, received, left_root, right_root, *state):
    square = pltpu.HBM((BLK, BLK), F32)
    return pl.pallas_call(
        block_kernel,
        in_specs=[SMEM, VMEM, VMEM, VMEM] + [HBM] * 4,
        out_specs=[VMEM] + [HBM] * 4,
        out_shape=[jax.ShapeDtypeStruct((BLK, BLK), BF16)] + [square] * 4,
        scratch_shapes=[pltpu.VMEM((BLK, BLK), F32)] * 4 + [pltpu.SemaphoreType.DMA((8,))],
        compiler_params=params(),
        cost_estimate=pl.CostEstimate(flops=2**31, bytes_accessed=11 * 2**20, transcendentals=0),
        name="block_step",
    )(refresh, received, left_root, right_root, *[in_hbm(a) for a in state])


def body(inputs, norm_gain, cotangent, owners, refresh, left_stats, right_stats, left_inverse, right_inverse):
    xl = lax.axis_index("xl").reshape(1)
    owner = owners[0]
    tokens, width = inputs.shape
    count = lax.axis_size(FSDP) * width
    peers = lax.axis_size(("z", "core"))

    features = lax.all_gather(prepare(inputs, norm_gain), ("z", "core"), axis=0, tiled=True)
    values = inputs.astype(F32)
    squares = jnp.sum(values * values, axis=1).reshape(1, tokens)
    roots = pack_roots(left_inverse, right_inverse)
    squares_other = lax.ppermute(squares, "xl", SWAP)
    roots = lax.all_to_all(roots, GROUP, split_axis=0, concat_axis=0, tiled=True)
    roots, other, squares, squares_other = lax.optimization_barrier((roots, cotangent, squares, squares_other))
    other = lax.ppermute(other, "xl", SWAP)
    squares = jnp.broadcast_to(squares + squares_other, (peers, tokens))
    squares = lax.all_to_all(squares, ("z", "core"), split_axis=0, concat_axis=0, tiled=True)
    scale = lax.rsqrt(jnp.sum(squares, axis=0, keepdims=True) / count + NORM_EPSILON)
    roots = pick(owner, roots)
    roots, scale = lax.optimization_barrier((roots, scale))
    roots = lax.all_to_all(roots, GROUP, split_axis=0, concat_axis=0, tiled=True)

    pieces = partials(xl, features, scaled(scale, cotangent))
    pieces, other = lax.optimization_barrier((pieces, other))
    pieces = partials(1 - xl, features, other, scale, pieces)
    shape = pieces.shape
    pieces, roots = lax.optimization_barrier((pieces.reshape(2 * N_GROUP, *shape[2:]), roots))
    pieces = lax.all_to_all(pieces, ("y", "xh", "xl"), split_axis=0, concat_axis=0, tiled=True)
    grads = route(owner, pieces.reshape(shape))
    grads = lax.all_to_all(grads, GROUP, split_axis=0, concat_axis=0, tiled=True)
    left_root, right_root = unpack_roots(roots)
    state = (left_stats, right_stats, left_inverse, right_inverse)
    return tuple(block_step(refresh, grads, left_root, right_root, *state))


def solution(mesh):
    split = Mesh(mesh.devices.reshape(4, 2, 2, 8, 2), ("y", "xh", "xl", "z", "core"))
    both = P(GROUP, FSDP)
    in_specs = (both, P(FSDP), both, P(FSDP, None), both, both, both, both, both)
    return jax.shard_map(body, mesh=split, in_specs=in_specs, out_specs=(both,) * 5, check_vma=False)
```

```python
import jax
import jax.numpy as jnp
from jax import lax
from jax.experimental import pallas as pl
from jax.experimental.pallas import tpu as pltpu
from jax.sharding import Mesh
from jax.sharding import PartitionSpec as P

NORM_EPSILON = 1e-05
SCALE_EPSILON = 1e-06
DECAY_RATE = 0.95
RIDGE_TERM = 1e-06
BLK = 512
N_GROUP = 8
LOAD = 512
CHUNK = BLK // N_GROUP
PACKED = CHUNK + 16
GROUP = ("y", "xh")
TURNED = ("xh", "y")
FSDP = ("xl", "z", "core")
SWAP = [(0, 1), (1, 0)]
BF16 = jnp.bfloat16
F32 = jnp.float32
NT = (((1,), (1,)), ((), ()))
TN = (((0,), (0,)), ((), ()))
HBM = pl.BlockSpec(memory_space=pltpu.HBM)
VMEM = pl.BlockSpec(memory_space=pltpu.VMEM)
SMEM = pl.BlockSpec(memory_space=pltpu.SMEM)


def turned(group):
    return (group & 1) * (N_GROUP // 2) + (group >> 1)


def in_hbm(x):
    return pltpu.with_memory_space_constraint(x, pltpu.HBM)


def params():
    return pltpu.CompilerParams(vmem_limit_bytes=48 * 2**20)


def dot(a, b):
    return jnp.dot(a, b, preferred_element_type=F32)


def dot_dims(a, b, dims):
    return lax.dot_general(a, b, dims, preferred_element_type=F32)


def split2(a):
    high = a.astype(BF16)
    return high, (a - high.astype(F32)).astype(BF16)


def prepare_kernel(x_ref, gain_ref, xt_ref):
    xt_ref[...] = (x_ref[...].astype(F32) * gain_ref[...].astype(F32)).astype(BF16).T


def prepare(x, gain):
    tokens, width = x.shape
    step = tokens // 2
    return pl.pallas_call(
        prepare_kernel,
        grid=(2,),
        in_specs=[pl.BlockSpec((step, width), lambda i: (i, 0)), pl.BlockSpec((1, width), lambda i: (0, 0))],
        out_specs=pl.BlockSpec((width, step), lambda i: (0, i)),
        out_shape=pltpu.HBM((width, tokens), BF16),
        name="prepare",
    )(x, gain.reshape(1, width))


def triangle():
    rows = lax.broadcasted_iota(jnp.int32, (BLK, BLK), 0)
    cols = lax.broadcasted_iota(jnp.int32, (BLK, BLK), 1)
    return rows, cols


def pack_roots_kernel(l_ref, r_ref, o_ref, left, right, sems):
    copies = [pltpu.make_async_copy(l_ref, left, sems.at[0]), pltpu.make_async_copy(r_ref, right, sems.at[1])]
    for copy in copies:
        copy.start()
    for copy in copies:
        copy.wait()
    rows, cols = triangle()
    packed = jnp.where(cols > rows, left[...], right[...]).astype(BF16)
    diagonal = jnp.sum(jnp.where(cols == rows, left[...], 0.0), axis=0, keepdims=True)
    diagonal = jnp.broadcast_to(diagonal, (PACKED - CHUNK, BLK)).astype(BF16)
    for i in range(N_GROUP):
        o_ref[i, :CHUNK] = packed[i * CHUNK : (i + 1) * CHUNK]
        o_ref[i, CHUNK:] = diagonal


def pack_roots(left, right):
    return pl.pallas_call(
        pack_roots_kernel,
        in_specs=[HBM, HBM],
        out_specs=VMEM,
        out_shape=pltpu.HBM((N_GROUP, PACKED, BLK), BF16),
        scratch_shapes=[pltpu.VMEM((BLK, BLK), F32)] * 2 + [pltpu.SemaphoreType.DMA((2,))],
        compiler_params=params(),
        name="pack_roots",
    )(in_hbm(left), in_hbm(right))


def pick_kernel(owner_ref, x_ref, o_ref):
    for i in range(N_GROUP):
        o_ref[turned(i)] = x_ref[turned(owner_ref[i])]


def pick(owner, x):
    return pl.pallas_call(
        pick_kernel,
        in_specs=[SMEM, VMEM],
        out_specs=VMEM,
        out_shape=pltpu.HBM(x.shape, x.dtype),
        compiler_params=params(),
        name="pick",
    )(owner, x)


def unpack_roots_kernel(x_ref, l_ref, r_ref):
    rows, cols = triangle()
    packed = jnp.concatenate([x_ref[i, :CHUNK] for i in range(N_GROUP)], axis=0).astype(F32)
    upper = jnp.where(cols > rows, packed, 0.0)
    lower = jnp.where(cols < rows, packed, 0.0)
    diagonal = x_ref[0, CHUNK:].astype(F32)[:1]
    l_ref[...] = (upper + upper.T + jnp.where(cols == rows, diagonal, 0.0)).astype(BF16)
    r_ref[...] = (packed - upper + lower.T).astype(BF16)


def unpack_roots(x):
    square = jax.ShapeDtypeStruct((BLK, BLK), BF16)
    return pl.pallas_call(
        unpack_roots_kernel,
        in_specs=[VMEM],
        out_specs=[VMEM, VMEM],
        out_shape=[square, square],
        compiler_params=params(),
        name="unpack_roots",
    )(x)


def column_of(scale_ref):
    return jnp.broadcast_to(scale_ref[...], (8, scale_ref.shape[1])).T[:, :1]


def scale_kernel(scale_ref, x_ref, o_ref):
    o_ref[...] = (x_ref[...].astype(F32) * column_of(scale_ref)).astype(BF16)


def scaled(scale, x):
    return pl.pallas_call(
        scale_kernel,
        in_specs=[VMEM, VMEM],
        out_specs=VMEM,
        out_shape=pltpu.HBM(x.shape, BF16),
        compiler_params=params(),
        name="scaled",
    )(scale, x)


def partials_kernel(place_ref, x_ref, cot_ref, *refs):
    *rest, o_ref, local, scaled_ref, part_ref, sems = refs
    rows, tokens = local.shape
    slabs, pieces = rows // BLK, rows // LOAD
    loads = [
        pltpu.make_async_copy(x_ref.at[pl.ds(n * LOAD, LOAD)], local.at[pl.ds(n * LOAD, LOAD)], sems.at[n])
        for n in range(pieces)
    ]
    spans = [pl.ds(first, BLK) for first in range(0, tokens, BLK)]
    cots = [
        pltpu.make_async_copy(cot_ref.at[span], scaled_ref.at[span], sems.at[pieces + n])
        for n, span in enumerate(spans)
    ]
    stores = [
        pltpu.make_async_copy(part_ref.at[i], o_ref.at[place_ref[0], :, i], sems.at[pieces + len(spans) + i])
        for i in range(slabs)
    ]
    for load in loads[: BLK // LOAD]:
        load.start()
    if not rest:
        for copy in cots:
            copy.start()
    for load in loads[BLK // LOAD :]:
        load.start()
    if rest:
        column = column_of(rest[0])
        for span in spans:
            scaled_ref[span] = (cot_ref[span].astype(F32) * column[span.start : span.start + BLK]).astype(BF16)
    else:
        for copy in cots:
            copy.wait()
    for i in range(slabs):
        for load in loads[i * (BLK // LOAD) : (i + 1) * (BLK // LOAD)]:
            load.wait()
        part = dot(local[i * BLK : (i + 1) * BLK], scaled_ref[...]).astype(BF16)
        for j in range(N_GROUP):
            part_ref[i, j] = part[j * CHUNK : (j + 1) * CHUNK]
        stores[i].start()
    for store in stores:
        store.wait()


def partials(place, x, cot, *rest):
    rows, tokens = x.shape
    slabs = rows // BLK
    return pl.pallas_call(
        partials_kernel,
        in_specs=[SMEM, HBM] + ([VMEM, VMEM, HBM] if rest else [HBM]),
        out_specs=HBM,
        scratch_shapes=[
            pltpu.VMEM((rows, tokens), BF16),
            pltpu.VMEM((tokens, BLK), BF16),
            pltpu.VMEM((slabs, N_GROUP, CHUNK, BLK), BF16),
            pltpu.SemaphoreType.DMA((rows // LOAD + tokens // BLK + slabs,)),
        ],
        out_shape=pltpu.HBM((2, N_GROUP, slabs, CHUNK, BLK), BF16),
        input_output_aliases={4: 0} if rest else {},
        compiler_params=params(),
        cost_estimate=pl.CostEstimate(flops=2 * rows * tokens * BLK, bytes_accessed=12 * 2**20, transcendentals=0),
        name="partials",
    )(place, in_hbm(x), cot if rest else in_hbm(cot), *rest)


def route_kernel(owner_ref, x_ref, o_ref):
    for half in range(2):
        for n in range(x_ref.shape[2]):
            value = x_ref[half, 0, n].astype(F32)
            for g in range(1, N_GROUP):
                value = value + x_ref[half, g, n].astype(F32)
            value = value.astype(BF16)
            slab = half * x_ref.shape[2] + n
            o_ref[turned(slab), 1] = value
            o_ref[turned(owner_ref[slab]), 0] = value


def route(owner, x):
    return pl.pallas_call(
        route_kernel,
        in_specs=[SMEM, VMEM],
        out_specs=VMEM,
        out_shape=pltpu.HBM((N_GROUP, 2, CHUNK, BLK), BF16),
        compiler_params=params(),
        name="route",
    )(owner, x)


def inverse_fourth_root(statistic):
    rows, cols = triangle()
    eye = (rows == cols).astype(F32)
    matrix = statistic + RIDGE_TERM * eye
    scaling = 2.5 * lax.rsqrt(jnp.sum(matrix * matrix, keepdims=True))
    matrix = scaling * matrix
    rounded = matrix.astype(BF16)
    product = dot(rounded, rounded)
    square = (1.5625 * eye - 0.625 * matrix + 0.0625 * product).astype(BF16)
    once = (1.25 * matrix - 0.25 * product).astype(BF16)
    fourth = dot(square, square).astype(BF16)
    return jnp.sqrt(jnp.sqrt(scaling)) * (1.5625 * eye - 0.3125 * matrix - 0.25 * dot(fourth, once))


def block_kernel(
    refresh_ref, u_ref, lroot_ref, rroot_ref, ls_ref, rs_ref, li_ref, ri_ref,
    upd_ref, la_ref, ra_ref, ln_ref, rn_ref, left, right, left_new, right_new, sems,
):
    fresh = refresh_ref[0, 0] > 0
    loads = [pltpu.make_async_copy(ls_ref, left, sems.at[0]), pltpu.make_async_copy(rs_ref, right, sems.at[1])]
    keeps = [pltpu.make_async_copy(li_ref, left_new, sems.at[2]), pltpu.make_async_copy(ri_ref, right_new, sems.at[3])]
    stores = [pltpu.make_async_copy(left, la_ref, sems.at[4]), pltpu.make_async_copy(right, ra_ref, sems.at[5])]
    news = [pltpu.make_async_copy(left_new, ln_ref, sems.at[6]), pltpu.make_async_copy(right_new, rn_ref, sems.at[7])]
    for load in loads:
        load.start()

    @pl.when(jnp.logical_not(fresh))
    def _():
        for keep in keeps:
            keep.start()

    grad, natural = (jnp.concatenate([u_ref[turned(g), n] for g in range(N_GROUP)], axis=0) for n in range(2))
    for n, (accum, dims) in enumerate(((left, NT), (right, TN))):
        gram = dot_dims(grad, grad, dims)
        loads[n].wait()
        accum[...] = DECAY_RATE * accum[...] + (1.0 - DECAY_RATE) * gram
        stores[n].start()

    @pl.when(fresh)
    def _():
        for accum, new, copy in ((left, left_new, news[0]), (right, right_new, news[1])):
            new[...] = inverse_fourth_root(accum[...])
            copy.start()

    @pl.when(jnp.logical_not(fresh))
    def _():
        for keep, copy in zip(keeps, news):
            keep.wait()
            copy.start()

    right_root = rroot_ref[...]
    high, low = split2(dot(lroot_ref[...], natural))
    conditioned = dot(high, right_root) + dot(low, right_root)
    mean = jnp.sum(conditioned * conditioned, keepdims=True) * (1.0 / (BLK * BLK))
    upd_ref[...] = (conditioned * lax.rsqrt(mean + SCALE_EPSILON)).astype(BF16)
    for copy in stores + news:
        copy.wait()


def block_step(refresh, received, left_root, right_root, *state):
    square = pltpu.HBM((BLK, BLK), F32)
    return pl.pallas_call(
        block_kernel,
        in_specs=[SMEM, VMEM, VMEM, VMEM] + [HBM] * 4,
        out_specs=[VMEM] + [HBM] * 4,
        out_shape=[jax.ShapeDtypeStruct((BLK, BLK), BF16)] + [square] * 4,
        scratch_shapes=[pltpu.VMEM((BLK, BLK), F32)] * 4 + [pltpu.SemaphoreType.DMA((8,))],
        compiler_params=params(),
        cost_estimate=pl.CostEstimate(flops=2**31, bytes_accessed=11 * 2**20, transcendentals=0),
        name="block_step",
    )(refresh, received, left_root, right_root, *[in_hbm(a) for a in state])


def body(inputs, norm_gain, cotangent, owners, refresh, left_stats, right_stats, left_inverse, right_inverse):
    xl = lax.axis_index("xl").reshape(1)
    owner = owners[0]
    tokens, width = inputs.shape
    count = lax.axis_size(FSDP) * width
    peers = lax.axis_size(("z", "core"))

    features = lax.all_gather(prepare(inputs, norm_gain), ("z", "core"), axis=0, tiled=True)
    values = inputs.astype(F32)
    squares = jnp.sum(values * values, axis=1).reshape(1, tokens)
    roots = pack_roots(left_inverse, right_inverse)
    squares_other = lax.ppermute(squares, "xl", SWAP)
    roots = lax.all_to_all(roots, TURNED, split_axis=0, concat_axis=0, tiled=True)
    roots, other, squares, squares_other = lax.optimization_barrier((roots, cotangent, squares, squares_other))
    other = lax.ppermute(other, "xl", SWAP)
    squares = jnp.broadcast_to(squares + squares_other, (peers, tokens))
    squares = lax.all_to_all(squares, ("z", "core"), split_axis=0, concat_axis=0, tiled=True)
    scale = lax.rsqrt(jnp.sum(squares, axis=0, keepdims=True) / count + NORM_EPSILON)
    roots = pick(owner, roots)
    roots, scale = lax.optimization_barrier((roots, scale))
    roots = lax.all_to_all(roots, TURNED, split_axis=0, concat_axis=0, tiled=True)

    pieces = partials(xl, features, scaled(scale, cotangent))
    pieces, other = lax.optimization_barrier((pieces, other))
    pieces = partials(1 - xl, features, other, scale, pieces)
    shape = pieces.shape
    pieces, roots = lax.optimization_barrier((pieces.reshape(2 * N_GROUP, *shape[2:]), roots))
    pieces = lax.all_to_all(pieces, ("xl", "y", "xh"), split_axis=0, concat_axis=0, tiled=True)
    grads = route(owner, pieces.reshape(shape))
    grads = lax.all_to_all(grads, TURNED, split_axis=0, concat_axis=0, tiled=True)
    left_root, right_root = unpack_roots(roots)
    state = (left_stats, right_stats, left_inverse, right_inverse)
    return tuple(block_step(refresh, grads, left_root, right_root, *state))


def solution(mesh):
    split = Mesh(mesh.devices.reshape(4, 2, 2, 8, 2), ("y", "xh", "xl", "z", "core"))
    both = P(GROUP, FSDP)
    in_specs = (both, P(FSDP), both, P(FSDP, None), both, both, both, both, both)
    return jax.shard_map(body, mesh=split, in_specs=in_specs, out_specs=(both,) * 5, check_vma=False)
```

```python
import jax
import jax.numpy as jnp
from jax import lax
from jax.experimental import pallas as pl
from jax.experimental.pallas import tpu as pltpu
from jax.sharding import Mesh
from jax.sharding import PartitionSpec as P

NORM_EPSILON = 1e-05
SCALE_EPSILON = 1e-06
DECAY_RATE = 0.95
RIDGE_TERM = 1e-06
BLK = 512
N_GROUP = 8
STEPS = 2
CHUNK = BLK // N_GROUP
PACKED = CHUNK + 16
GROUP = ("y", "xh")
TURNED = ("xh", "y")
FSDP = ("xl", "z", "core")
SWAP = [(0, 1), (1, 0)]
BF16 = jnp.bfloat16
F32 = jnp.float32
NT = (((1,), (1,)), ((), ()))
TN = (((0,), (0,)), ((), ()))
HBM = pl.BlockSpec(memory_space=pltpu.HBM)
VMEM = pl.BlockSpec(memory_space=pltpu.VMEM)
SMEM = pl.BlockSpec(memory_space=pltpu.SMEM)


def turned(group):
    return (group & 1) * (N_GROUP // 2) + (group >> 1)


def in_hbm(x):
    return pltpu.with_memory_space_constraint(x, pltpu.HBM)


def params():
    return pltpu.CompilerParams(vmem_limit_bytes=48 * 2**20)


def dot(a, b):
    return jnp.dot(a, b, preferred_element_type=F32)


def dot_dims(a, b, dims):
    return lax.dot_general(a, b, dims, preferred_element_type=F32)


def split2(a):
    high = a.astype(BF16)
    return high, (a - high.astype(F32)).astype(BF16)


def prepare_kernel(x_ref, gain_ref, xt_ref):
    xt_ref[...] = (x_ref[...].astype(F32) * gain_ref[...].astype(F32)).astype(BF16).T


def prepare(x, gain):
    tokens, width = x.shape
    step = tokens // STEPS
    return pl.pallas_call(
        prepare_kernel,
        grid=(STEPS,),
        in_specs=[pl.BlockSpec((step, width), lambda i: (i, 0)), pl.BlockSpec((1, width), lambda i: (0, 0))],
        out_specs=pl.BlockSpec((width, step), lambda i: (0, i)),
        out_shape=pltpu.HBM((width, tokens), BF16),
        name="prepare",
    )(x, gain.reshape(1, width))


def triangle():
    rows = lax.broadcasted_iota(jnp.int32, (BLK, BLK), 0)
    cols = lax.broadcasted_iota(jnp.int32, (BLK, BLK), 1)
    return rows, cols


def pack_roots_kernel(l_ref, r_ref, o_ref, left, right, sems):
    copies = [pltpu.make_async_copy(l_ref, left, sems.at[0]), pltpu.make_async_copy(r_ref, right, sems.at[1])]
    for copy in copies:
        copy.start()
    for copy in copies:
        copy.wait()
    rows, cols = triangle()
    packed = jnp.where(cols > rows, left[...], right[...]).astype(BF16)
    diagonal = jnp.sum(jnp.where(cols == rows, left[...], 0.0), axis=0, keepdims=True)
    diagonal = jnp.broadcast_to(diagonal, (PACKED - CHUNK, BLK)).astype(BF16)
    for i in range(N_GROUP):
        o_ref[i, :CHUNK] = packed[i * CHUNK : (i + 1) * CHUNK]
        o_ref[i, CHUNK:] = diagonal


def pack_roots(left, right):
    return pl.pallas_call(
        pack_roots_kernel,
        in_specs=[HBM, HBM],
        out_specs=VMEM,
        out_shape=pltpu.HBM((N_GROUP, PACKED, BLK), BF16),
        scratch_shapes=[pltpu.VMEM((BLK, BLK), F32)] * 2 + [pltpu.SemaphoreType.DMA((2,))],
        compiler_params=params(),
        name="pack_roots",
    )(in_hbm(left), in_hbm(right))


def pick_kernel(owner_ref, x_ref, o_ref):
    for i in range(N_GROUP):
        o_ref[turned(i)] = x_ref[turned(owner_ref[i])]


def pick(owner, x):
    return pl.pallas_call(
        pick_kernel,
        in_specs=[SMEM, VMEM],
        out_specs=VMEM,
        out_shape=pltpu.HBM(x.shape, x.dtype),
        compiler_params=params(),
        name="pick",
    )(owner, x)


def unpack_roots_kernel(x_ref, l_ref, r_ref):
    rows, cols = triangle()
    packed = jnp.concatenate([x_ref[i, :CHUNK] for i in range(N_GROUP)], axis=0).astype(F32)
    upper = jnp.where(cols > rows, packed, 0.0)
    lower = jnp.where(cols < rows, packed, 0.0)
    diagonal = x_ref[0, CHUNK:].astype(F32)[:1]
    l_ref[...] = (upper + upper.T + jnp.where(cols == rows, diagonal, 0.0)).astype(BF16)
    r_ref[...] = (packed - upper + lower.T).astype(BF16)


def unpack_roots(x):
    square = jax.ShapeDtypeStruct((BLK, BLK), BF16)
    return pl.pallas_call(
        unpack_roots_kernel,
        in_specs=[VMEM],
        out_specs=[VMEM, VMEM],
        out_shape=[square, square],
        compiler_params=params(),
        name="unpack_roots",
    )(x)


def column_of(scale_ref):
    return jnp.broadcast_to(scale_ref[...], (8, scale_ref.shape[1])).T[:, :1]


def scale_kernel(scale_ref, x_ref, o_ref):
    o_ref[...] = (x_ref[...].astype(F32) * column_of(scale_ref)).astype(BF16)


def scaled(scale, x):
    return pl.pallas_call(
        scale_kernel,
        in_specs=[VMEM, VMEM],
        out_specs=VMEM,
        out_shape=pltpu.HBM(x.shape, BF16),
        compiler_params=params(),
        name="scaled",
    )(scale, x)


def partials_kernel(place_ref, x_ref, cot_ref, *refs):
    *rest, o_ref, local, scaled_ref, part_ref, sems = refs
    rows, tokens = local.shape
    slabs, pieces = rows // BLK, rows // BLK - 1 + tokens // BLK
    spans = [pl.ds(first, BLK) for first in range(0, tokens, BLK)]
    parts = [(pl.ds(0, BLK), span) for span in spans]
    parts += [(pl.ds(first, BLK), pl.ds(0, tokens)) for first in range(BLK, rows, BLK)]
    loads = [pltpu.make_async_copy(x_ref.at[at], local.at[at], sems.at[n]) for n, at in enumerate(parts)]
    cots = [
        pltpu.make_async_copy(cot_ref.at[span], scaled_ref.at[span], sems.at[pieces + n])
        for n, span in enumerate(spans)
    ]
    stores = [
        pltpu.make_async_copy(part_ref.at[i], o_ref.at[place_ref[0], :, i], sems.at[pieces + len(spans) + i])
        for i in range(slabs)
    ]
    for n, span in enumerate(spans):
        loads[n].start()
        if not rest:
            cots[n].start()
    for load in loads[len(spans) :]:
        load.start()
    column = column_of(rest[0]) if rest else None
    part = jnp.zeros((BLK, BLK), F32)
    for n, span in enumerate(spans):
        if rest:
            scaled_ref[span] = (cot_ref[span].astype(F32) * column[span.start : span.start + BLK]).astype(BF16)
        else:
            cots[n].wait()
        loads[n].wait()
        part = part + dot(local[:BLK, span], scaled_ref[span])
    for i in range(slabs):
        if i > 0:
            loads[len(spans) + i - 1].wait()
            part = dot(local[i * BLK : (i + 1) * BLK], scaled_ref[...])
        part = part.astype(BF16)
        for j in range(N_GROUP):
            part_ref[i, j] = part[j * CHUNK : (j + 1) * CHUNK]
        stores[i].start()
    for store in stores:
        store.wait()


def partials(place, x, cot, *rest):
    rows, tokens = x.shape
    slabs = rows // BLK
    return pl.pallas_call(
        partials_kernel,
        in_specs=[SMEM, HBM] + ([VMEM, VMEM, HBM] if rest else [HBM]),
        out_specs=HBM,
        scratch_shapes=[
            pltpu.VMEM((rows, tokens), BF16),
            pltpu.VMEM((tokens, BLK), BF16),
            pltpu.VMEM((slabs, N_GROUP, CHUNK, BLK), BF16),
            pltpu.SemaphoreType.DMA((2 * slabs - 1 + 2 * tokens // BLK,)),
        ],
        out_shape=pltpu.HBM((2, N_GROUP, slabs, CHUNK, BLK), BF16),
        input_output_aliases={4: 0} if rest else {},
        compiler_params=params(),
        cost_estimate=pl.CostEstimate(flops=2 * rows * tokens * BLK, bytes_accessed=12 * 2**20, transcendentals=0),
        name="partials",
    )(place, in_hbm(x), cot if rest else in_hbm(cot), *rest)


def route_kernel(owner_ref, x_ref, o_ref):
    for half in range(2):
        for n in range(x_ref.shape[2]):
            value = x_ref[half, 0, n].astype(F32)
            for g in range(1, N_GROUP):
                value = value + x_ref[half, g, n].astype(F32)
            value = value.astype(BF16)
            slab = half * x_ref.shape[2] + n
            o_ref[turned(slab), 1] = value
            o_ref[turned(owner_ref[slab]), 0] = value


def route(owner, x):
    return pl.pallas_call(
        route_kernel,
        in_specs=[SMEM, VMEM],
        out_specs=VMEM,
        out_shape=pltpu.HBM((N_GROUP, 2, CHUNK, BLK), BF16),
        compiler_params=params(),
        name="route",
    )(owner, x)


def inverse_fourth_roots(statistics):
    rows, cols = triangle()
    eye = (rows == cols).astype(F32)
    matrices = [statistic + RIDGE_TERM * eye for statistic in statistics]
    scalings = [2.5 * lax.rsqrt(jnp.sum(matrix * matrix, keepdims=True)) for matrix in matrices]
    matrices = [scaling * matrix for scaling, matrix in zip(scalings, matrices)]
    rounded = [matrix.astype(BF16) for matrix in matrices]
    products = [dot(matrix, matrix) for matrix in rounded]
    pairs = list(zip(matrices, products))
    squares = [(1.5625 * eye - 0.625 * matrix + 0.0625 * product).astype(BF16) for matrix, product in pairs]
    once = [(1.25 * matrix - 0.25 * product).astype(BF16) for matrix, product in pairs]
    fourths = [dot(square, square).astype(BF16) for square in squares]
    lasts = [dot(fourth, factor) for fourth, factor in zip(fourths, once)]
    return [
        jnp.sqrt(jnp.sqrt(scaling)) * (1.5625 * eye - 0.3125 * matrix - 0.25 * last)
        for scaling, matrix, last in zip(scalings, matrices, lasts)
    ]


def block_kernel(
    refresh_ref, u_ref, lroot_ref, rroot_ref, ls_ref, rs_ref, li_ref, ri_ref,
    upd_ref, la_ref, ra_ref, ln_ref, rn_ref, left, right, left_new, right_new, sems,
):
    fresh = refresh_ref[0, 0] > 0
    loads = [pltpu.make_async_copy(ls_ref, left, sems.at[0]), pltpu.make_async_copy(rs_ref, right, sems.at[1])]
    keeps = [pltpu.make_async_copy(li_ref, left_new, sems.at[2]), pltpu.make_async_copy(ri_ref, right_new, sems.at[3])]
    stores = [pltpu.make_async_copy(left, la_ref, sems.at[4]), pltpu.make_async_copy(right, ra_ref, sems.at[5])]
    news = [pltpu.make_async_copy(left_new, ln_ref, sems.at[6]), pltpu.make_async_copy(right_new, rn_ref, sems.at[7])]
    for load in loads:
        load.start()

    @pl.when(jnp.logical_not(fresh))
    def _():
        for keep in keeps:
            keep.start()

    grad, natural = (jnp.concatenate([u_ref[turned(g), n] for g in range(N_GROUP)], axis=0) for n in range(2))
    for n, (accum, dims) in enumerate(((left, NT), (right, TN))):
        gram = dot_dims(grad, grad, dims)
        loads[n].wait()
        accum[...] = DECAY_RATE * accum[...] + (1.0 - DECAY_RATE) * gram
        stores[n].start()

    @pl.when(fresh)
    def _():
        values = inverse_fourth_roots([left[...], right[...]])
        for value, new, copy in zip(values, (left_new, right_new), news):
            new[...] = value
            copy.start()

    @pl.when(jnp.logical_not(fresh))
    def _():
        for keep, copy in zip(keeps, news):
            keep.wait()
            copy.start()

    right_root = rroot_ref[...]
    high, low = split2(dot(lroot_ref[...], natural))
    conditioned = dot(high, right_root) + dot(low, right_root)
    mean = jnp.sum(conditioned * conditioned, keepdims=True) * (1.0 / (BLK * BLK))
    upd_ref[...] = (conditioned * lax.rsqrt(mean + SCALE_EPSILON)).astype(BF16)
    for copy in stores + news:
        copy.wait()


def block_step(refresh, received, left_root, right_root, *state):
    square = pltpu.HBM((BLK, BLK), F32)
    return pl.pallas_call(
        block_kernel,
        in_specs=[SMEM, VMEM, VMEM, VMEM] + [HBM] * 4,
        out_specs=[VMEM] + [HBM] * 4,
        out_shape=[jax.ShapeDtypeStruct((BLK, BLK), BF16)] + [square] * 4,
        scratch_shapes=[pltpu.VMEM((BLK, BLK), F32)] * 4 + [pltpu.SemaphoreType.DMA((8,))],
        compiler_params=params(),
        cost_estimate=pl.CostEstimate(flops=2**31, bytes_accessed=11 * 2**20, transcendentals=0),
        name="block_step",
    )(refresh, received, left_root, right_root, *[in_hbm(a) for a in state])


def body(inputs, norm_gain, cotangent, owners, refresh, left_stats, right_stats, left_inverse, right_inverse):
    xl = lax.axis_index("xl").reshape(1)
    owner = owners[0]
    tokens, width = inputs.shape
    count = lax.axis_size(FSDP) * width
    peers = lax.axis_size(("z", "core"))

    features = lax.all_gather(prepare(inputs, norm_gain), ("z", "core"), axis=0, tiled=True)
    values = inputs.astype(F32)
    squares = jnp.sum(values * values, axis=1).reshape(1, tokens)
    roots = pack_roots(left_inverse, right_inverse)
    squares_other = lax.ppermute(squares, "xl", SWAP)
    roots = lax.all_to_all(roots, TURNED, split_axis=0, concat_axis=0, tiled=True)
    roots, other, squares, squares_other = lax.optimization_barrier((roots, cotangent, squares, squares_other))
    other = lax.ppermute(other, "xl", SWAP)
    squares = jnp.broadcast_to(squares + squares_other, (peers, tokens))
    squares = lax.all_to_all(squares, ("z", "core"), split_axis=0, concat_axis=0, tiled=True)
    scale = lax.rsqrt(jnp.sum(squares, axis=0, keepdims=True) / count + NORM_EPSILON)
    roots = pick(owner, roots)
    roots, scale = lax.optimization_barrier((roots, scale))
    roots = lax.all_to_all(roots, TURNED, split_axis=0, concat_axis=0, tiled=True)

    pieces = partials(xl, features, scaled(scale, cotangent))
    pieces, other = lax.optimization_barrier((pieces, other))
    pieces = partials(1 - xl, features, other, scale, pieces)
    shape = pieces.shape
    pieces, roots = lax.optimization_barrier((pieces.reshape(2 * N_GROUP, *shape[2:]), roots))
    pieces = lax.all_to_all(pieces, ("xl", "y", "xh"), split_axis=0, concat_axis=0, tiled=True)
    grads = route(owner, pieces.reshape(shape))
    grads = lax.all_to_all(grads, TURNED, split_axis=0, concat_axis=0, tiled=True)
    left_root, right_root = unpack_roots(roots)
    state = (left_stats, right_stats, left_inverse, right_inverse)
    return tuple(block_step(refresh, grads, left_root, right_root, *state))


def solution(mesh):
    split = Mesh(mesh.devices.reshape(4, 2, 2, 8, 2), ("y", "xh", "xl", "z", "core"))
    both = P(GROUP, FSDP)
    in_specs = (both, P(FSDP), both, P(FSDP, None), both, both, both, both, both)
    return jax.shard_map(body, mesh=split, in_specs=in_specs, out_specs=(both,) * 5, check_vma=False)
```

```python
import jax
import jax.numpy as jnp
from jax import lax
from jax.experimental import pallas as pl
from jax.experimental.pallas import tpu as pltpu
from jax.sharding import Mesh
from jax.sharding import PartitionSpec as P

NORM_EPSILON = 1e-05
SCALE_EPSILON = 1e-06
DECAY_RATE = 0.95
RIDGE_TERM = 1e-06
BLK = 512
N_GROUP = 8
CHUNK = BLK // N_GROUP
PACKED = CHUNK + 16
GROUP = ("y", "xh")
TURNED = ("xh", "y")
FSDP = ("xl", "z", "core")
SWAP = [(0, 1), (1, 0)]
BF16 = jnp.bfloat16
F32 = jnp.float32
NT = (((1,), (1,)), ((), ()))
TN = (((0,), (0,)), ((), ()))
HBM = pl.BlockSpec(memory_space=pltpu.HBM)
VMEM = pl.BlockSpec(memory_space=pltpu.VMEM)
SMEM = pl.BlockSpec(memory_space=pltpu.SMEM)


def turned(group):
    return (group & 1) * (N_GROUP // 2) + (group >> 1)


def in_hbm(x):
    return pltpu.with_memory_space_constraint(x, pltpu.HBM)


def params():
    return pltpu.CompilerParams(vmem_limit_bytes=48 * 2**20)


def dot(a, b):
    return jnp.dot(a, b, preferred_element_type=F32)


def dot_dims(a, b, dims):
    return lax.dot_general(a, b, dims, preferred_element_type=F32)


def split2(a):
    high = a.astype(BF16)
    return high, (a - high.astype(F32)).astype(BF16)


def prepare_kernel(x_ref, gain_ref, xt_ref, local, turned_ref, gain_local, sems):
    spans = [pl.ds(n * BLK, BLK) for n in range(local.shape[0] // BLK)]
    count = len(spans)
    loads = [pltpu.make_async_copy(x_ref.at[s], local.at[s], sems.at[n]) for n, s in enumerate(spans)]
    stores = [pltpu.make_async_copy(turned_ref.at[:, s], xt_ref.at[:, s], sems.at[count + n]) for n, s in enumerate(spans)]
    gain_load = pltpu.make_async_copy(gain_ref, gain_local, sems.at[2 * count])
    gain_load.start()
    for load in loads:
        load.start()
    gain_load.wait()
    gain = gain_local[...].astype(F32)
    for n, span in enumerate(spans):
        loads[n].wait()
        turned_ref[:, span] = (local[span].astype(F32) * gain).astype(BF16).T
        stores[n].start()
    for store in stores:
        store.wait()


def prepare(x, gain):
    tokens, width = x.shape
    return pl.pallas_call(
        prepare_kernel,
        in_specs=[HBM, HBM],
        out_specs=HBM,
        out_shape=pltpu.HBM((width, tokens), BF16),
        scratch_shapes=[
            pltpu.VMEM((tokens, width), BF16),
            pltpu.VMEM((width, tokens), BF16),
            pltpu.VMEM((1, width), BF16),
            pltpu.SemaphoreType.DMA((2 * tokens // BLK + 1,)),
        ],
        compiler_params=params(),
        name="prepare",
    )(in_hbm(x), in_hbm(gain.reshape(1, width)))


def triangle():
    rows = lax.broadcasted_iota(jnp.int32, (BLK, BLK), 0)
    cols = lax.broadcasted_iota(jnp.int32, (BLK, BLK), 1)
    return rows, cols


def pack_roots_kernel(l_ref, r_ref, o_ref, left, right, sems):
    copies = [pltpu.make_async_copy(l_ref, left, sems.at[0]), pltpu.make_async_copy(r_ref, right, sems.at[1])]
    for copy in copies:
        copy.start()
    for copy in copies:
        copy.wait()
    rows, cols = triangle()
    packed = jnp.where(cols > rows, left[...], right[...]).astype(BF16)
    diagonal = jnp.sum(jnp.where(cols == rows, left[...], 0.0), axis=0, keepdims=True)
    diagonal = jnp.broadcast_to(diagonal, (PACKED - CHUNK, BLK)).astype(BF16)
    for i in range(N_GROUP):
        o_ref[i, :CHUNK] = packed[i * CHUNK : (i + 1) * CHUNK]
        o_ref[i, CHUNK:] = diagonal


def pack_roots(left, right):
    return pl.pallas_call(
        pack_roots_kernel,
        in_specs=[HBM, HBM],
        out_specs=VMEM,
        out_shape=pltpu.HBM((N_GROUP, PACKED, BLK), BF16),
        scratch_shapes=[pltpu.VMEM((BLK, BLK), F32)] * 2 + [pltpu.SemaphoreType.DMA((2,))],
        compiler_params=params(),
        name="pack_roots",
    )(in_hbm(left), in_hbm(right))


def pick_kernel(owner_ref, x_ref, o_ref):
    for i in range(N_GROUP):
        o_ref[turned(i)] = x_ref[turned(owner_ref[i])]


def pick(owner, x):
    return pl.pallas_call(
        pick_kernel,
        in_specs=[SMEM, VMEM],
        out_specs=VMEM,
        out_shape=pltpu.HBM(x.shape, x.dtype),
        compiler_params=params(),
        name="pick",
    )(owner, x)


def unpack_roots_kernel(x_ref, l_ref, r_ref):
    rows, cols = triangle()
    packed = jnp.concatenate([x_ref[i, :CHUNK] for i in range(N_GROUP)], axis=0).astype(F32)
    upper = jnp.where(cols > rows, packed, 0.0)
    lower = jnp.where(cols < rows, packed, 0.0)
    diagonal = x_ref[0, CHUNK:].astype(F32)[:1]
    l_ref[...] = (upper + upper.T + jnp.where(cols == rows, diagonal, 0.0)).astype(BF16)
    r_ref[...] = (packed - upper + lower.T).astype(BF16)


def unpack_roots(x):
    square = jax.ShapeDtypeStruct((BLK, BLK), BF16)
    return pl.pallas_call(
        unpack_roots_kernel,
        in_specs=[VMEM],
        out_specs=[VMEM, VMEM],
        out_shape=[square, square],
        compiler_params=params(),
        name="unpack_roots",
    )(x)


def column_of(scale_ref):
    return jnp.broadcast_to(scale_ref[...], (8, scale_ref.shape[1])).T[:, :1]


def scale_kernel(scale_ref, x_ref, o_ref):
    o_ref[...] = (x_ref[...].astype(F32) * column_of(scale_ref)).astype(BF16)


def scaled(scale, x):
    return pl.pallas_call(
        scale_kernel,
        in_specs=[VMEM, VMEM],
        out_specs=VMEM,
        out_shape=pltpu.HBM(x.shape, BF16),
        compiler_params=params(),
        name="scaled",
    )(scale, x)


def partials_kernel(place_ref, x_ref, cot_ref, *refs):
    *rest, o_ref, local, scaled_ref, part_ref, sems = refs
    rows, tokens = local.shape
    slabs, pieces = rows // BLK, rows // BLK - 1 + tokens // BLK
    spans = [pl.ds(first, BLK) for first in range(0, tokens, BLK)]
    parts = [(pl.ds(0, BLK), span) for span in spans]
    parts += [(pl.ds(first, BLK), pl.ds(0, tokens)) for first in range(BLK, rows, BLK)]
    loads = [pltpu.make_async_copy(x_ref.at[at], local.at[at], sems.at[n]) for n, at in enumerate(parts)]
    cots = [
        pltpu.make_async_copy(cot_ref.at[span], scaled_ref.at[span], sems.at[pieces + n])
        for n, span in enumerate(spans)
    ]
    stores = [
        pltpu.make_async_copy(part_ref.at[i], o_ref.at[place_ref[0], :, i], sems.at[pieces + len(spans) + i])
        for i in range(slabs)
    ]
    for n, span in enumerate(spans):
        loads[n].start()
        if not rest:
            cots[n].start()
    for load in loads[len(spans) :]:
        load.start()
    column = column_of(rest[0]) if rest else None
    part = jnp.zeros((BLK, BLK), F32)
    for n, span in enumerate(spans):
        if rest:
            scaled_ref[span] = (cot_ref[span].astype(F32) * column[span.start : span.start + BLK]).astype(BF16)
        else:
            cots[n].wait()
        loads[n].wait()
        part = part + dot(local[:BLK, span], scaled_ref[span])
    for i in range(slabs):
        if i > 0:
            loads[len(spans) + i - 1].wait()
            part = dot(local[i * BLK : (i + 1) * BLK], scaled_ref[...])
        part = part.astype(BF16)
        for j in range(N_GROUP):
            part_ref[i, j] = part[j * CHUNK : (j + 1) * CHUNK]
        stores[i].start()
    for store in stores:
        store.wait()


def partials(place, x, cot, *rest):
    rows, tokens = x.shape
    slabs = rows // BLK
    return pl.pallas_call(
        partials_kernel,
        in_specs=[SMEM, HBM] + ([VMEM, VMEM, HBM] if rest else [HBM]),
        out_specs=HBM,
        scratch_shapes=[
            pltpu.VMEM((rows, tokens), BF16),
            pltpu.VMEM((tokens, BLK), BF16),
            pltpu.VMEM((slabs, N_GROUP, CHUNK, BLK), BF16),
            pltpu.SemaphoreType.DMA((2 * slabs - 1 + 2 * tokens // BLK,)),
        ],
        out_shape=pltpu.HBM((2, N_GROUP, slabs, CHUNK, BLK), BF16),
        input_output_aliases={4: 0} if rest else {},
        compiler_params=params(),
        cost_estimate=pl.CostEstimate(flops=2 * rows * tokens * BLK, bytes_accessed=12 * 2**20, transcendentals=0),
        name="partials",
    )(place, in_hbm(x), cot if rest else in_hbm(cot), *rest)


def route_kernel(owner_ref, x_ref, o_ref, sums, sems):
    copies = []
    for half in range(2):
        for n in range(x_ref.shape[2]):
            value = x_ref[half, 0, n].astype(F32)
            for g in range(1, N_GROUP):
                value = value + x_ref[half, g, n].astype(F32)
            slab = half * x_ref.shape[2] + n
            sums[slab] = value.astype(BF16)
            for kind, dest in enumerate((turned(owner_ref[slab]), turned(slab))):
                copies.append(pltpu.make_async_copy(sums.at[slab], o_ref.at[dest, kind], sems.at[2 * slab + kind]))
                copies[-1].start()
    for copy in copies:
        copy.wait()


def route(owner, x):
    return pl.pallas_call(
        route_kernel,
        in_specs=[SMEM, VMEM],
        out_specs=HBM,
        out_shape=pltpu.HBM((N_GROUP, 2, CHUNK, BLK), BF16),
        scratch_shapes=[pltpu.VMEM((N_GROUP, CHUNK, BLK), BF16), pltpu.SemaphoreType.DMA((2 * N_GROUP,))],
        compiler_params=params(),
        name="route",
    )(owner, x)


def inverse_fourth_roots(statistics):
    rows, cols = triangle()
    eye = (rows == cols).astype(F32)
    matrices = [statistic + RIDGE_TERM * eye for statistic in statistics]
    scalings = [2.5 * lax.rsqrt(jnp.sum(matrix * matrix, keepdims=True)) for matrix in matrices]
    matrices = [scaling * matrix for scaling, matrix in zip(scalings, matrices)]
    rounded = [matrix.astype(BF16) for matrix in matrices]
    products = [dot(matrix, matrix) for matrix in rounded]
    pairs = list(zip(matrices, products))
    squares = [(1.5625 * eye - 0.625 * matrix + 0.0625 * product).astype(BF16) for matrix, product in pairs]
    once = [(1.25 * matrix - 0.25 * product).astype(BF16) for matrix, product in pairs]
    fourths = [dot(square, square).astype(BF16) for square in squares]
    lasts = [dot(fourth, factor) for fourth, factor in zip(fourths, once)]
    return [
        jnp.sqrt(jnp.sqrt(scaling)) * (1.5625 * eye - 0.3125 * matrix - 0.25 * last)
        for scaling, matrix, last in zip(scalings, matrices, lasts)
    ]


def block_kernel(
    refresh_ref, u_ref, lroot_ref, rroot_ref, ls_ref, rs_ref, li_ref, ri_ref,
    upd_ref, la_ref, ra_ref, ln_ref, rn_ref, left, right, left_new, right_new, sems,
):
    fresh = refresh_ref[0, 0] > 0
    loads = [pltpu.make_async_copy(ls_ref, left, sems.at[0]), pltpu.make_async_copy(rs_ref, right, sems.at[1])]
    keeps = [pltpu.make_async_copy(li_ref, left_new, sems.at[2]), pltpu.make_async_copy(ri_ref, right_new, sems.at[3])]
    stores = [pltpu.make_async_copy(left, la_ref, sems.at[4]), pltpu.make_async_copy(right, ra_ref, sems.at[5])]
    news = [pltpu.make_async_copy(left_new, ln_ref, sems.at[6]), pltpu.make_async_copy(right_new, rn_ref, sems.at[7])]
    for load in loads:
        load.start()

    @pl.when(jnp.logical_not(fresh))
    def _():
        for keep in keeps:
            keep.start()

    grad, natural = (jnp.concatenate([u_ref[turned(g), n] for g in range(N_GROUP)], axis=0) for n in range(2))
    for n, (accum, dims) in enumerate(((left, NT), (right, TN))):
        gram = dot_dims(grad, grad, dims)
        loads[n].wait()
        accum[...] = DECAY_RATE * accum[...] + (1.0 - DECAY_RATE) * gram
        stores[n].start()

    @pl.when(fresh)
    def _():
        values = inverse_fourth_roots([left[...], right[...]])
        for value, new, copy in zip(values, (left_new, right_new), news):
            new[...] = value
            copy.start()

    @pl.when(jnp.logical_not(fresh))
    def _():
        for keep, copy in zip(keeps, news):
            keep.wait()
            copy.start()

    right_root = rroot_ref[...]
    high, low = split2(dot(lroot_ref[...], natural))
    conditioned = dot(high, right_root) + dot(low, right_root)
    mean = jnp.sum(conditioned * conditioned, keepdims=True) * (1.0 / (BLK * BLK))
    upd_ref[...] = (conditioned * lax.rsqrt(mean + SCALE_EPSILON)).astype(BF16)
    for copy in stores + news:
        copy.wait()


def block_step(refresh, received, left_root, right_root, *state):
    square = pltpu.HBM((BLK, BLK), F32)
    return pl.pallas_call(
        block_kernel,
        in_specs=[SMEM, VMEM, VMEM, VMEM] + [HBM] * 4,
        out_specs=[VMEM] + [HBM] * 4,
        out_shape=[jax.ShapeDtypeStruct((BLK, BLK), BF16)] + [square] * 4,
        scratch_shapes=[pltpu.VMEM((BLK, BLK), F32)] * 4 + [pltpu.SemaphoreType.DMA((8,))],
        compiler_params=params(),
        cost_estimate=pl.CostEstimate(flops=2**31, bytes_accessed=11 * 2**20, transcendentals=0),
        name="block_step",
    )(refresh, received, left_root, right_root, *[in_hbm(a) for a in state])


def body(inputs, norm_gain, cotangent, owners, refresh, left_stats, right_stats, left_inverse, right_inverse):
    xl = lax.axis_index("xl").reshape(1)
    owner = owners[0]
    tokens, width = inputs.shape
    count = lax.axis_size(FSDP) * width
    peers = lax.axis_size(("z", "core"))

    features = lax.all_gather(prepare(inputs, norm_gain), ("z", "core"), axis=0, tiled=True)
    values = inputs.astype(F32)
    squares = jnp.sum(values * values, axis=1).reshape(1, tokens)
    roots = pack_roots(left_inverse, right_inverse)
    squares_other = lax.ppermute(squares, "xl", SWAP)
    roots = lax.all_to_all(roots, TURNED, split_axis=0, concat_axis=0, tiled=True)
    roots, other, squares, squares_other = lax.optimization_barrier((roots, cotangent, squares, squares_other))
    other = lax.ppermute(other, "xl", SWAP)
    squares = jnp.broadcast_to(squares + squares_other, (peers, tokens))
    squares = lax.all_to_all(squares, ("z", "core"), split_axis=0, concat_axis=0, tiled=True)
    scale = lax.rsqrt(jnp.sum(squares, axis=0, keepdims=True) / count + NORM_EPSILON)
    roots = pick(owner, roots)
    roots, scale = lax.optimization_barrier((roots, scale))
    roots = lax.all_to_all(roots, TURNED, split_axis=0, concat_axis=0, tiled=True)

    pieces = partials(xl, features, scaled(scale, cotangent))
    pieces, other = lax.optimization_barrier((pieces, other))
    pieces = partials(1 - xl, features, other, scale, pieces)
    shape = pieces.shape
    pieces, roots = lax.optimization_barrier((pieces.reshape(2 * N_GROUP, *shape[2:]), roots))
    pieces = lax.all_to_all(pieces, ("xl", "y", "xh"), split_axis=0, concat_axis=0, tiled=True)
    grads = route(owner, pieces.reshape(shape))
    grads = lax.all_to_all(grads, TURNED, split_axis=0, concat_axis=0, tiled=True)
    left_root, right_root = unpack_roots(roots)
    state = (left_stats, right_stats, left_inverse, right_inverse)
    return tuple(block_step(refresh, grads, left_root, right_root, *state))


def solution(mesh):
    split = Mesh(mesh.devices.reshape(4, 2, 2, 8, 2), ("y", "xh", "xl", "z", "core"))
    both = P(GROUP, FSDP)
    in_specs = (both, P(FSDP), both, P(FSDP, None), both, both, both, both, both)
    return jax.shard_map(body, mesh=split, in_specs=in_specs, out_specs=(both,) * 5, check_vma=False)
```
